128 devices in a mesh: rows: 32 (over x, z, core), cols: 4 (over y).
Axes of the slice: x: 4, y: 4, z: 4, core: 2. Of those that a mesh axis runs over, the one named last changes fastest.
Arguments:
- points: float32 [98304, 1024], P('rows', 'cols'), may hold values from -80 to 80
- codes: int32 [128, 98304], P('cols', 'rows'), may hold values from 0 to 255, as said below
- rotation: float32 [1024, 1024], P('rows', 'cols'), may hold values from -0.16 to 1.16
Outputs:
- new_rotation: float32 [1024, 1024], P('rows', 'cols')
- centroids: float32 [128, 2048], P('cols')
The draws below stay inside these ranges and needn't reach their ends.
Inputs may be any that keep to these rules, and one draw needn't show every extreme that they name: For every subspace, the first 256 vectors hold each of the 256 codes once.
All inputs are finite; a program needn't handle non-finite values.
Results may differ from the reference program's by a relative error of at most 0.00011.
Values sent between devices are 32-bit elements; how exact they have to be, the bound alone decides.
No kernel may reach another device: no remote copies, remote signals or barrier semaphores. Data moves between devices by JAX's collectives and lax.ppermute only.
A program may use at most 128 MiB of HBM per device.

```python
import jax
import jax.numpy as jnp
from jax import lax

D = 1024
M = 128
K = 256
NS_ITERS = 6
SUB = 8
TOTAL = 98304


def shared_codes(key):
    base = jax.random.fold_in(key, 11)
    key_raw, key_offset = jax.random.split(base)
    position = jnp.arange(TOTAL, dtype=jnp.int32)
    spread = K - 2 * K // 3 * position // TOTAL
    raw_codes = jax.random.randint(key_raw, (M, TOTAL), 0, 1 << 20, dtype=jnp.int32)
    drawn = raw_codes % spread[None, :]
    offsets = jax.random.randint(key_offset, (M, 1), 0, K, dtype=jnp.int32)
    cyclic = (position[None, :] + offsets) % K
    return jnp.where(position[None, :] < K, cyclic, drawn).astype(jnp.int32)


def draw_codes(key, part):
    return shared_codes(key)


def draw_points(key, part):
    code_table = shared_codes(key)
    table = jnp.clip(jax.random.normal(jax.random.fold_in(key, 12), (M, K, SUB), jnp.float32), -5.0, 5.0)
    centers = table[jnp.arange(M)[:, None], code_table]
    centers = centers.transpose(1, 0, 2).reshape(TOTAL, D)
    noise = jnp.clip(jax.random.normal(jax.random.fold_in(key, 14), (TOTAL, D), jnp.float32), -5.0, 5.0)
    unit = jax.random.uniform(jax.random.fold_in(key, 13), (D,), jnp.float32)
    feature_scale = jnp.exp(unit * jnp.log(3.0))
    return ((centers + 0.6 * noise) * feature_scale[None, :]).astype(jnp.float32)


def draw_rotation(key, part):
    noise = jnp.clip(jax.random.normal(jax.random.fold_in(key, 15), (D, D), jnp.float32), -5.0, 5.0)
    index_range = jnp.arange(D, dtype=jnp.int32)
    identity = (index_range[:, None] == index_range[None, :]).astype(jnp.float32)
    spread = 0.35
    return (identity + spread * noise / D ** 0.5).astype(jnp.float32)


def setup_inputs(seed: int = 0) -> dict:
    splits = jax.random.split(jax.random.key(seed), 4)
    return {
        "points": draw_points(jax.random.fold_in(splits[3], 71), 0),
        "codes": draw_codes(jax.random.fold_in(splits[3], 71), 0),
        "rotation": draw_rotation(jax.random.fold_in(splits[3], 71), 0),
    }


def reference(points, codes, rotation):
    highest = lax.Precision.HIGHEST
    rotated = jnp.dot(points, rotation, precision=highest, preferred_element_type=jnp.float32)
    blocks = rotated.reshape(TOTAL, M, SUB).transpose(1, 0, 2)

    def one_subspace(item):
        block, code_row = item
        sums_here = jax.ops.segment_sum(block, code_row, K)
        counts_here = jax.ops.segment_sum(jnp.ones((TOTAL,), jnp.float32), code_row, K)
        centers = sums_here / counts_here[:, None]
        return (centers, centers[code_row])
    centers_all, recon_all = lax.map(one_subspace, (blocks, codes))
    approx = recon_all.transpose(1, 0, 2).reshape(TOTAL, D)
    cross = jnp.dot(points.T, approx, precision=highest, preferred_element_type=jnp.float32)
    iterate = 1.7 * cross / jnp.sqrt(jnp.sum(cross * cross) + 1e-06)
    for step_index in range(NS_ITERS):
        gram = jnp.dot(iterate.T, iterate, precision=highest, preferred_element_type=jnp.float32)
        iterate = 1.5 * iterate - 0.5 * jnp.dot(iterate, gram, precision=highest, preferred_element_type=jnp.float32)
    new_rotation = iterate * D ** 0.5
    return (new_rotation, centers_all.reshape(M, K * SUB))
```

```python
import jax
import jax.numpy as jnp
from jax import lax
from jax.experimental import pallas as pl
from jax.experimental.pallas import tpu as pltpu
from jax.sharding import Mesh, PartitionSpec as P

D = 1024
M = 128
K = 256
NS_ITERS = 6
SUB = 8
ROWS = ("x", "z", "core")
OWNERS = ("y", "x", "z", "core")
BF16 = jnp.bfloat16
F32 = jnp.float32
NN = (((1,), (0,)), ((), ()))
NT = (((1,), (1,)), ((), ()))


def split(value):
    high = value.astype(BF16)
    return high, (value - high.astype(F32)).astype(BF16)


def mxu(left, right, dims):
    return lax.dot_general(left, right, dims, preferred_element_type=F32)


def dot3(left_high, left_low, right_high, right_low, dims):
    return (
        mxu(left_high, right_high, dims)
        + mxu(left_high, right_low, dims)
        + mxu(left_low, right_high, dims)
    )


def spread_to(value, axes, count):
    copies = jnp.broadcast_to(value[None], (count,) + value.shape)
    return lax.all_to_all(copies, axes, 0, 0, tiled=True)


def sums_kernel(y_ref, pts_ref, rot_ref, c0, c1, c2, c3, out_ref, rotated_ref, ph_ref, pl_ref):
    count = pts_ref.shape[0]
    ph, plo = split(pts_ref[...])
    ph_ref[...] = ph
    pl_ref[...] = plo
    y = y_ref[0]

    def rotate(j, carry):
        panel = rot_ref[:, pl.ds(pl.multiple_of(j * 256, 256), 256)].T
        rh, rl = split(panel)
        part = dot3(rh, rl, ph_ref[...], pl_ref[...], NT)
        rotated_ref[pl.ds(j * 32, 32)] = part.reshape(32, SUB, count)
        return carry

    lax.fori_loop(0, D // 256, rotate, 0)

    step = 512
    rows16 = lax.broadcasted_iota(jnp.int32, (16, step), 0).astype(F32)
    marks = [(rows16 + 16.0 * t).astype(BF16) for t in range(4)]
    one = jnp.ones((16, step), BF16)
    zero = jnp.zeros((16, step), BF16)
    lane = lax.broadcasted_iota(jnp.int32, (SUB, 128), 1)
    for i, codes_ref in enumerate((c0, c1, c2, c3)):
        block = lax.rem(y + 4 - i, 4)

        def group(eight, half_group, codes_ref, block):
            total = jnp.zeros((256, 256), F32)
            g = eight * 2 + half_group
            for n in range(0, count, step):
                lefts, rights = [], []
                rows = codes_ref[pl.ds(pl.multiple_of(eight * 8, 8), 8), n : n + step]
                for mm in range(4):
                    row = rows[half_group * 4 + mm : half_group * 4 + mm + 1]
                    low = jnp.broadcast_to((row & 63).astype(F32), (16, step)).astype(BF16)
                    top = jnp.broadcast_to((row >> 6).astype(F32), (16, step)).astype(BF16)
                    value = rotated_ref[block * 32 + g * 4 + mm, :, n : n + step]
                    high = value.astype(BF16).astype(F32)
                    both = jnp.concatenate([high, value - high], axis=0).astype(BF16)
                    for t in range(4):
                        lefts.append(jnp.where(top == jnp.full((16, step), t, BF16), both, zero))
                        rights.append(jnp.where(low == marks[t], one, zero))
                total += mxu(
                    jnp.concatenate(lefts, axis=0), jnp.concatenate(rights, axis=0), NT
                )
            for mm in range(4):
                slab = total[mm * 64 : mm * 64 + 64, (mm // 2) * 128 : (mm // 2) * 128 + 128]
                parts = [
                    slab[t * 16 : t * 16 + 8] + slab[t * 16 + 8 : t * 16 + 16] for t in range(4)
                ]
                for half in range(2):
                    even, odd = parts[half * 2], parts[half * 2 + 1]
                    if mm % 2 == 0:
                        odd = pltpu.roll(odd, 64, axis=1)
                    else:
                        even = pltpu.roll(even, 64, axis=1)
                    out_ref[block * 32 + g * 4 + mm, :, half * 128 : half * 128 + 128] = jnp.where(
                        lane < 64, even, odd
                    )

        def eight_rows(eight, carry, codes_ref=codes_ref, block=block):
            group(eight, 0, codes_ref, block)
            group(eight, 1, codes_ref, block)
            return carry

        lax.fori_loop(0, 4, eight_rows, 0)


def code_sums(y, points, panel, codes):
    count = points.shape[0]
    vmem = pl.BlockSpec(memory_space=pltpu.VMEM)
    return pl.pallas_call(
        sums_kernel,
        out_shape=jax.ShapeDtypeStruct((M, SUB, K), F32),
        in_specs=[pl.BlockSpec(memory_space=pltpu.SMEM)] + [vmem] * 6,
        out_specs=vmem,
        scratch_shapes=[
            pltpu.VMEM((M, SUB, count), F32),
            pltpu.VMEM((count, 256), BF16),
            pltpu.VMEM((count, 256), BF16),
        ],
        compiler_params=pltpu.CompilerParams(vmem_limit_bytes=56 * 1024 * 1024),
        name="code_sums",
    )(y, points, panel, *codes)


def cross_kernel(y_ref, pts_ref, tab_ref, c0, c1, c2, c3, out_ref, ah_ref, al_ref, ph_ref, pl_ref):
    count = pts_ref.shape[0]
    ph, plo = split(pts_ref[...])
    ph_ref[...] = ph
    pl_ref[...] = plo
    y = y_ref[0]
    for i, codes_ref in enumerate((c0, c1, c2, c3)):
        block = lax.rem(y + 4 - i, 4)

        def pair(eight, two, codes_ref, block):
            g = eight * 4 + two
            tables = [tab_ref[block * 32 + g * 2 + mm] for mm in range(2)]
            for n in range(0, count, 128):
                found = []
                rows = codes_ref[pl.ds(pl.multiple_of(eight * 8, 8), 8), n : n + 128]
                for mm in range(2):
                    row = rows[two * 2 + mm : two * 2 + mm + 1]
                    index = jnp.broadcast_to(row, (SUB, 128))
                    table = tables[mm]
                    inner = index & 127
                    first = jnp.take_along_axis(
                        table[:, :128], inner, axis=1, mode="promise_in_bounds"
                    )
                    second = jnp.take_along_axis(
                        table[:, 128:], inner, axis=1, mode="promise_in_bounds"
                    )
                    found.append(jnp.where(index < 128, first, second))
                high, low = split(jnp.concatenate(found, axis=0))
                ah_ref[pl.ds(pl.multiple_of(g * 16, 16), 16), n : n + 128] = high
                al_ref[pl.ds(pl.multiple_of(g * 16, 16), 16), n : n + 128] = low

        def eight_rows(eight, carry, codes_ref=codes_ref, block=block):
            for two in range(4):
                pair(eight, two, codes_ref, block)
            return carry

        lax.fori_loop(0, 4, eight_rows, 0)
        out_ref[pl.ds(pl.multiple_of(block * 256, 256), 256), :] = dot3(
            ah_ref[...], al_ref[...], ph_ref[...], pl_ref[...], NN
        )


def cross_part(y, points, table, codes):
    count = points.shape[0]
    vmem = pl.BlockSpec(memory_space=pltpu.VMEM)
    return pl.pallas_call(
        cross_kernel,
        out_shape=jax.ShapeDtypeStruct((D, 256), F32),
        in_specs=[pl.BlockSpec(memory_space=pltpu.SMEM)] + [vmem] * 6,
        out_specs=vmem,
        scratch_shapes=[
            pltpu.VMEM((256, count), BF16),
            pltpu.VMEM((256, count), BF16),
            pltpu.VMEM((count, 256), BF16),
            pltpu.VMEM((count, 256), BF16),
        ],
        compiler_params=pltpu.CompilerParams(vmem_limit_bytes=56 * 1024 * 1024),
        name="cross_part",
    )(y, points, table, *codes)


def shards(points, codes, rotation):
    y = lax.axis_index("y")
    y_scalar = y.astype(jnp.int32).reshape(1)
    all_codes = [codes] + [
        lax.ppermute(codes, "y", [(s, (s + i) % 4) for s in range(4)]) for i in (1, 2, 3)
    ]
    swapped = lax.ppermute(
        rotation, ("x", "y"), [(a * 4 + b, b * 4 + a) for a in range(4) for b in range(4)]
    )
    pieces = spread_to(swapped, ROWS, 32).reshape(4, 8, 32, 256)
    panel = pieces.transpose(1, 2, 0, 3).reshape(256, D)
    local_counts = jnp.sum(
        (codes[:, :, None] == jnp.arange(K, dtype=jnp.int32)).astype(F32), axis=1
    )
    counts = lax.psum(local_counts, ROWS)

    sums = code_sums(y_scalar, points, panel, all_codes)
    owned = jnp.sum(lax.all_to_all(sums, OWNERS, 0, 0, tiled=True), axis=0)
    own_row = lax.axis_index(ROWS)
    own_counts = lax.dynamic_slice_in_dim(counts, own_row, 1, axis=0)
    centers = owned / own_counts
    table = spread_to(centers, OWNERS, 128)
    mine = lax.dynamic_slice_in_dim(table, y * 32, 32, axis=0)
    centroids = mine.transpose(0, 2, 1).reshape(32, K * SUB)

    cross = cross_part(y_scalar, points, table, all_codes)
    block = jnp.sum(
        lax.all_to_all(cross.reshape(32, 32, 256), ROWS, 0, 0, tiled=True), axis=0
    )
    whole = spread_to(block, ROWS + ("y",), 128)
    whole = whole.reshape(32, 4, 32, 256).transpose(0, 2, 1, 3).reshape(D, D)
    iterate = 1.7 * whole / jnp.sqrt(jnp.sum(whole * whole) + 1e-06)
    for step_index in range(NS_ITERS):
        gram = lax.dot_general(iterate, iterate, NT, precision=lax.Precision.HIGH, preferred_element_type=F32)
        iterate = 1.5 * iterate - 0.5 * lax.dot_general(
            gram, iterate, NN, precision=lax.Precision.HIGH, preferred_element_type=F32
        )
    out = lax.dynamic_slice(iterate, (y * 256, own_row * 32), (256, 32)).T
    return (out * D**0.5, centroids)


def solution(mesh):
    grid = Mesh(mesh.devices.reshape(4, 4, 2, 4), ("x", "z", "core", "y"))
    in_specs = (P(ROWS, "y"), P("y", ROWS), P(ROWS, "y"))
    out_specs = (P(ROWS, "y"), P("y", None))
    return jax.shard_map(shards, mesh=grid, in_specs=in_specs, out_specs=out_specs, check_vma=False)
```

```python
import jax
import jax.numpy as jnp
from jax import lax
from jax.experimental import pallas as pl
from jax.experimental.pallas import tpu as pltpu
from jax.sharding import Mesh, PartitionSpec as P

D = 1024
M = 128
K = 256
NS_ITERS = 6
SUB = 8
ROWS = ("x", "z", "core")
CHIPS = ("y", "x", "z")
BF16 = jnp.bfloat16
F32 = jnp.float32
NN = (((1,), (0,)), ((), ()))
NT = (((1,), (1,)), ((), ()))
VMEM = pl.BlockSpec(memory_space=pltpu.VMEM)
SMEM = pl.BlockSpec(memory_space=pltpu.SMEM)
PARAMS = pltpu.CompilerParams(vmem_limit_bytes=56 * 1024 * 1024)
PAYLOAD = K + 128


def split(value):
    high = value.astype(BF16)
    return high, (value - high.astype(F32)).astype(BF16)


def mxu(left, right, dims):
    return lax.dot_general(left, right, dims, preferred_element_type=F32)


def dot3(left_high, left_low, right_high, right_low, dims):
    return (
        mxu(left_high, right_high, dims)
        + mxu(left_high, right_low, dims)
        + mxu(left_low, right_high, dims)
    )


def spread_to(value, axes, count):
    copies = jnp.broadcast_to(value[None], (count,) + value.shape)
    return lax.all_to_all(copies, axes, 0, 0, tiled=True)


def swap_core(value):
    return lax.ppermute(value, "core", [(0, 1), (1, 0)])


def at8(index):
    return pl.ds(pl.multiple_of(index * 8, 8), 8)


def place_codes(where, y, c0, c1, c2, c3):
    for i, codes_ref in enumerate((c0, c1, c2, c3)):
        block = lax.rem(y + 4 - i, 4)
        where[pl.ds(pl.multiple_of(block * 32, 32), 32), :] = codes_ref[...]


def sums_kernel(
    place_ref, pts_ref, mine_ref, other_ref, c0, c1, c2, c3,
    keep_ref, give_ref, codes_ref, panel_ref, rotated_ref, ph_ref, pl_ref,
):
    count = pts_ref.shape[0]
    y, core = place_ref[0], place_ref[1]
    place_codes(codes_ref, y, c0, c1, c2, c3)
    ph, plo = split(pts_ref[...])
    ph_ref[...] = ph
    pl_ref[...] = plo
    for a in range(4):
        for z in range(4):
            columns = slice(a * 256, a * 256 + 256)
            first = pl.multiple_of(z * 64 + core * 32, 32)
            second = pl.multiple_of(z * 64 + (1 - core) * 32, 32)
            panel_ref[pl.ds(first, 32), columns] = mine_ref[a * 4 + z]
            panel_ref[pl.ds(second, 32), columns] = other_ref[a * 4 + z]

    def rotate(j, carry):
        panel = panel_ref[:, pl.ds(pl.multiple_of(j * 256, 256), 256)].T
        rh, rl = split(panel)
        part = dot3(rh, rl, ph_ref[...], pl_ref[...], NT)
        rotated_ref[pl.ds(j * 32, 32)] = part.reshape(32, SUB, count)
        return carry

    lax.fori_loop(0, D // 256, rotate, 0)

    step = 512
    rows16 = lax.broadcasted_iota(jnp.int32, (16, step), 0).astype(F32)
    marks = [(rows16 + 16.0 * t).astype(BF16) for t in range(4)]
    tops = [jnp.full((16, step), t, BF16) for t in range(4)]
    one = jnp.ones((16, step), BF16)
    zero = jnp.zeros((16, step), BF16)
    lane = lax.broadcasted_iota(jnp.int32, (SUB, 128), 1)

    def pick(even, odd, mm):
        if mm % 2 == 0:
            odd = pltpu.roll(odd, 64, axis=1)
        else:
            even = pltpu.roll(even, 64, axis=1)
        return jnp.where(lane < 64, even, odd)

    def group(eight, quad):
        total = jnp.zeros((288, 256), F32)
        for n in range(0, count, step):
            lefts, rights = [], []
            rows = codes_ref[at8(eight), n : n + step]
            for mm in range(4):
                row = rows[quad * 4 + mm : quad * 4 + mm + 1]
                low = jnp.broadcast_to((row & 63).astype(F32), (16, step)).astype(BF16)
                top = jnp.broadcast_to((row >> 6).astype(F32), (16, step)).astype(BF16)
                value = rotated_ref[eight * 8 + quad * 4 + mm, :, n : n + step]
                high = value.astype(BF16).astype(F32)
                both = jnp.concatenate([high, value - high], axis=0).astype(BF16)
                for t in range(4):
                    lefts.append(jnp.where(top == tops[t], both, zero))
                    rights.append(jnp.where(low == marks[t], one, zero))
            tall = (rows >> 6).astype(F32)
            tall = jnp.concatenate([tall, tall], axis=0).astype(BF16)
            for t in range(2):
                pattern = jnp.where(rows16 < 8, 2.0 * t, 2.0 * t + 1.0).astype(BF16)
                lefts.append(jnp.where(tall == pattern, one, zero))
            total += mxu(jnp.concatenate(lefts, axis=0), jnp.concatenate(rights, axis=0), NT)
        found = []
        for mm in range(4):
            columns = slice((mm // 2) * 128, (mm // 2) * 128 + 128)
            slab = total[mm * 64 : mm * 64 + 64, columns]
            parts = [slab[t * 16 : t * 16 + 8] + slab[t * 16 + 8 : t * 16 + 16] for t in range(4)]
            tally = [total[256 + t * 8 : 264 + t * 8, columns] for t in range(4)]
            halves = [pick(parts[2 * h], parts[2 * h + 1], mm) for h in range(2)]
            r = quad * 4 + mm
            ticks = [pick(tally[2 * h], tally[2 * h + 1], mm)[r : r + 1] for h in range(2)]
            ticks = jnp.concatenate(ticks + [jnp.zeros((6, 128), F32)], axis=0)
            found.append(jnp.concatenate(halves + [ticks], axis=1))
        for h in range(2):
            even, odd = found[2 * h], found[2 * h + 1]
            q = eight * 4 + quad * 2 + h
            keep_ref[q] = jnp.where(core == 0, even, odd)
            give_ref[q] = jnp.where(core == 0, odd, even)

    def eight_rows(eight, carry):
        group(eight, 0)
        group(eight, 1)
        return carry

    lax.fori_loop(0, M // 8, eight_rows, 0)


def code_sums(place, points, mine, other, codes):
    count = points.shape[0]
    half = jax.ShapeDtypeStruct((M // 2, SUB, PAYLOAD), F32)
    return pl.pallas_call(
        sums_kernel,
        out_shape=(half, half),
        in_specs=[SMEM] + [VMEM] * 7,
        out_specs=(VMEM, VMEM),
        scratch_shapes=[
            pltpu.VMEM((M, count), jnp.int32),
            pltpu.VMEM((256, D), F32),
            pltpu.VMEM((M, SUB, count), F32),
            pltpu.VMEM((count, 256), BF16),
            pltpu.VMEM((count, 256), BF16),
        ],
        compiler_params=PARAMS,
        name="code_sums",
    )(place, points, mine, other, *codes)


def cross_kernel(
    place_ref, pts_ref, mine_ref, other_ref, c0, c1, c2, c3,
    keep_ref, give_ref, codes_ref, tab_ref, ah_ref, al_ref, ph_ref, pl_ref,
):
    count = pts_ref.shape[0]
    y, core = place_ref[0], place_ref[1]
    place_codes(codes_ref, y, c0, c1, c2, c3)
    tab_ref[core] = mine_ref[...]
    tab_ref[1 - core] = other_ref[...]
    ph, plo = split(pts_ref[...])
    ph_ref[...] = ph
    pl_ref[...] = plo
    wide = 1024

    def look_up(block, eight):
        for n in range(0, count, wide):
            rows = codes_ref[at8(block * 4 + eight), n : n + wide]
            for two in range(4):
                both = []
                for mm in range(2):
                    index = jnp.broadcast_to(rows[two * 2 + mm : two * 2 + mm + 1], (SUB, wide))
                    table = tab_ref[mm, block * 16 + eight * 4 + two]
                    found = []
                    for k in range(0, wide, 128):
                        here = index[:, k : k + 128]
                        inner = here & 127
                        first = jnp.take_along_axis(
                            table[:, :128], inner, axis=1, mode="promise_in_bounds"
                        )
                        second = jnp.take_along_axis(
                            table[:, 128:], inner, axis=1, mode="promise_in_bounds"
                        )
                        found.append(jnp.where(here < 128, first, second))
                    both.append(jnp.concatenate(found, axis=1))
                high, low = split(jnp.concatenate(both, axis=0))
                place = pl.ds(pl.multiple_of(eight * 64 + two * 16, 16), 16)
                ah_ref[place, n : n + wide] = high
                al_ref[place, n : n + wide] = low

    def one_block(block, carry):
        def eight_rows(eight, inside):
            look_up(block, eight)
            return inside

        lax.fori_loop(0, 4, eight_rows, 0)
        part = dot3(ah_ref[...], al_ref[...], ph_ref[...], pl_ref[...], NN)
        for h in range(4):
            even = part[h * 64 : h * 64 + 32]
            odd = part[h * 64 + 32 : h * 64 + 64]
            keep_ref[block * 4 + h] = jnp.where(core == 0, even, odd)
            give_ref[block * 4 + h] = jnp.where(core == 0, odd, even)
        return carry

    lax.fori_loop(0, 4, one_block, 0)


def cross_part(place, points, mine, other, codes):
    count = points.shape[0]
    half = jax.ShapeDtypeStruct((16, 32, 256), F32)
    return pl.pallas_call(
        cross_kernel,
        out_shape=(half, half),
        in_specs=[SMEM] + [VMEM] * 7,
        out_specs=(VMEM, VMEM),
        scratch_shapes=[
            pltpu.VMEM((M, count), jnp.int32),
            pltpu.VMEM((2, M // 2, SUB, K), F32),
            pltpu.VMEM((256, count), BF16),
            pltpu.VMEM((256, count), BF16),
            pltpu.VMEM((count, 256), BF16),
            pltpu.VMEM((count, 256), BF16),
        ],
        compiler_params=PARAMS,
        name="cross_part",
    )(place, points, mine, other, *codes)


def iterate_kernel(place_ref, mine_ref, other_ref, out_ref, now_ref, hl_ref, gh_ref, gl_ref, tail_ref):
    y, column = place_ref[0], place_ref[2]
    total = jnp.zeros((1, 256), F32)
    for half, source in enumerate((mine_ref, other_ref)):
        for block in range(4):
            part = source[block * 16 : block * 16 + 16].reshape(512, 256)
            total += jnp.sum(part * part, axis=0, keepdims=True)
    scale = 1.7 / jnp.sqrt(jnp.sum(total, axis=1, keepdims=True) + 1e-06)
    for half, source in enumerate((mine_ref, other_ref)):
        for block in range(4):
            rows, columns = slice(half * 512, half * 512 + 512), slice(block * 256, block * 256 + 256)
            part = source[block * 16 : block * 16 + 16].reshape(512, 256) * scale
            now_ref[rows, columns] = part
            high, low = split(part)
            hl_ref[0, 0, rows, columns] = high
            hl_ref[0, 1, rows, columns] = low

    def step(k, carry):
        old, new = lax.rem(k, 2), 1 - lax.rem(k, 2)
        high_ref, low_ref = hl_ref.at[old, 0], hl_ref.at[old, 1]
        for j in range(4):
            strip, below = slice(j * 256, j * 256 + 256), slice(j * 256, D)
            gram = dot3(high_ref[below], low_ref[below], high_ref[strip], low_ref[strip], NT)
            high, low = split(gram)
            gh_ref[below, strip] = high
            gl_ref[below, strip] = low
            if j < 3:
                high, low = split(gram[256:].T)
                gh_ref[strip, j * 256 + 256 : D] = high
                gl_ref[strip, j * 256 + 256 : D] = low
        for j in range(4):
            strip = slice(j * 256, j * 256 + 256)
            moved = dot3(gh_ref[...], gl_ref[...], high_ref[:, strip], low_ref[:, strip], NN)
            value = 1.5 * now_ref[:, strip] - 0.5 * moved
            now_ref[:, strip] = value
            high, low = split(value)
            hl_ref[new, 0, :, strip] = high
            hl_ref[new, 1, :, strip] = low
        return carry

    lax.fori_loop(0, NS_ITERS - 1, step, 0)
    last = (NS_ITERS - 1) % 2
    high_ref, low_ref = hl_ref.at[last, 0], hl_ref.at[last, 1]
    columns = pl.ds(pl.multiple_of(column * 128, 128), 128)
    for half in range(2):
        rows = pl.ds(pl.multiple_of(half * 512 + y * 128, 128), 128)
        here = slice(half * 128, half * 128 + 128)
        tail_ref[0, here] = high_ref[rows]
        tail_ref[1, here] = low_ref[rows]
    gram = dot3(tail_ref[0], tail_ref[1], high_ref[...], low_ref[...], NT)
    high, low = split(gram)
    moved = dot3(high, low, high_ref[:, columns], low_ref[:, columns], NN)
    for half in range(2):
        rows = pl.ds(pl.multiple_of(half * 512 + y * 128, 128), 128)
        here = slice(half * 128, half * 128 + 128)
        out_ref[here, :] = (1.5 * now_ref[rows, columns] - 0.5 * moved[here]) * D**0.5


def newton_schulz(place, mine, other):
    return pl.pallas_call(
        iterate_kernel,
        out_shape=jax.ShapeDtypeStruct((256, 128), F32),
        in_specs=[SMEM, VMEM, VMEM],
        out_specs=VMEM,
        scratch_shapes=[
            pltpu.VMEM((D, D), F32),
            pltpu.VMEM((2, 2, D, D), BF16),
            pltpu.VMEM((D, D), BF16),
            pltpu.VMEM((D, D), BF16),
            pltpu.VMEM((2, 256, D), BF16),
        ],
        compiler_params=PARAMS,
        name="newton_schulz",
    )(place, mine, other)


def shards(points, codes, rotation):
    y, core = lax.axis_index("y"), lax.axis_index("core")
    own_row = lax.axis_index(ROWS)
    place = jnp.stack([y, core, own_row // 4]).astype(jnp.int32)
    all_codes = [codes] + [
        lax.ppermute(codes, "y", [(s, (s + i) % 4) for s in range(4)]) for i in (1, 2, 3)
    ]
    swapped = lax.ppermute(
        rotation, ("x", "y"), [(a * 4 + b, b * 4 + a) for a in range(4) for b in range(4)]
    )
    pieces = spread_to(swapped, ("x", "z"), 16)
    keep, give = code_sums(place, points, pieces, swap_core(pieces), all_codes)

    sums = keep + swap_core(give)
    sums = jnp.sum(lax.all_to_all(sums, CHIPS, 0, 0, tiled=True), axis=0)
    counts = 0.25 * sums[:2, K:].reshape(1, K)
    centers = spread_to(sums[:, :K] / counts, CHIPS, 64)
    others = swap_core(centers)

    keep, give = cross_part(place, points, centers, others, all_codes)
    block = keep + swap_core(give)
    block = jnp.sum(lax.all_to_all(block, ("x", "z"), 0, 0, tiled=True), axis=0)
    whole = spread_to(block, CHIPS, 64)
    result = newton_schulz(place, whole, swap_core(whole))

    result = lax.dynamic_slice_in_dim(result, (own_row % 4) * 32, 32, axis=1)
    result = result.reshape(2, 4, 32, 32)
    result = jnp.where(core == 0, result, result[::-1])
    rotated = result.transpose(3, 1, 0, 2).reshape(32, 256)

    ours = lax.dynamic_slice_in_dim(centers, y * 16, 16, axis=0)
    theirs = lax.dynamic_slice_in_dim(others, y * 16, 16, axis=0)
    first, second = jnp.where(core == 0, ours, theirs), jnp.where(core == 0, theirs, ours)
    centroids = jnp.stack([first, second], axis=1).transpose(0, 1, 3, 2).reshape(32, K * SUB)
    return (rotated, centroids)


def solution(mesh):
    grid = Mesh(mesh.devices.reshape(4, 4, 2, 4), ("x", "z", "core", "y"))
    in_specs = (P(ROWS, "y"), P("y", ROWS), P(ROWS, "y"))
    out_specs = (P(ROWS, "y"), P("y", None))
    return jax.shard_map(shards, mesh=grid, in_specs=in_specs, out_specs=out_specs, check_vma=False)
```

```python
import jax
import jax.numpy as jnp
from jax import lax
from jax.experimental import pallas as pl
from jax.experimental.pallas import tpu as pltpu
from jax.sharding import Mesh, PartitionSpec as P

D = 1024
M = 128
K = 256
NS_ITERS = 6
SUB = 8
ROWS = ("x", "z", "core")
CHIPS = ("y", "x", "z")
BF16 = jnp.bfloat16
F32 = jnp.float32
NN = (((1,), (0,)), ((), ()))
NT = (((1,), (1,)), ((), ()))
VMEM = pl.BlockSpec(memory_space=pltpu.VMEM)
SMEM = pl.BlockSpec(memory_space=pltpu.SMEM)
PARAMS = pltpu.CompilerParams(vmem_limit_bytes=56 * 1024 * 1024)
PAYLOAD = K + 128


def split(value):
    high = value.astype(BF16)
    return high, (value - high.astype(F32)).astype(BF16)


def mxu(left, right, dims):
    return lax.dot_general(left, right, dims, preferred_element_type=F32)


def dot3(left_high, left_low, right_high, right_low, dims):
    return (
        mxu(left_high, right_high, dims)
        + mxu(left_high, right_low, dims)
        + mxu(left_low, right_high, dims)
    )


def spread_to(value, axes, count):
    copies = jnp.broadcast_to(value[None], (count,) + value.shape)
    return lax.all_to_all(copies, axes, 0, 0, tiled=True)


def swap_core(value):
    return lax.ppermute(value, "core", [(0, 1), (1, 0)])


def at8(index):
    return pl.ds(pl.multiple_of(index * 8, 8), 8)


def place_codes(where, y, c0, c1, c2, c3):
    for i, codes_ref in enumerate((c0, c1, c2, c3)):
        block = lax.rem(y + 4 - i, 4)
        where[pl.ds(pl.multiple_of(block * 32, 32), 32), :] = codes_ref[...]


def sums_kernel(
    place_ref, pts_ref, pieces_ref, c0, c1, c2, c3,
    keep_ref, give_ref, codes_ref, panel_ref, rotated_ref, ph_ref, pl_ref,
):
    count = pts_ref.shape[0]
    y, core = place_ref[0], place_ref[1]
    place_codes(codes_ref, y, c0, c1, c2, c3)
    ph, plo = split(pts_ref[...])
    ph_ref[...] = ph
    pl_ref[...] = plo
    for a in range(4):
        for z in range(4):
            columns = slice(a * 256, a * 256 + 256)
            first = pl.multiple_of(z * 64 + core * 32, 32)
            second = pl.multiple_of(z * 64 + (1 - core) * 32, 32)
            panel_ref[pl.ds(first, 32), columns] = pieces_ref[a * 4 + z, 0]
            panel_ref[pl.ds(second, 32), columns] = pieces_ref[a * 4 + z, 1]

    def rotate(j, carry):
        panel = panel_ref[:, pl.ds(pl.multiple_of(j * 256, 256), 256)].T
        rh, rl = split(panel)
        part = dot3(rh, rl, ph_ref[...], pl_ref[...], NT)
        rotated_ref[pl.ds(j * 32, 32)] = part.reshape(32, SUB, count)
        return carry

    lax.fori_loop(0, D // 256, rotate, 0)

    step = 512
    rows16 = lax.broadcasted_iota(jnp.int32, (16, step), 0).astype(F32)
    marks = [(rows16 + 16.0 * t).astype(BF16) for t in range(4)]
    tops = [jnp.full((16, step), t, BF16) for t in range(4)]
    one = jnp.ones((16, step), BF16)
    zero = jnp.zeros((16, step), BF16)
    lane = lax.broadcasted_iota(jnp.int32, (SUB, 128), 1)

    def pick(even, odd, mm):
        if mm % 2 == 0:
            odd = pltpu.roll(odd, 64, axis=1)
        else:
            even = pltpu.roll(even, 64, axis=1)
        return jnp.where(lane < 64, even, odd)

    def group(eight, quad):
        total = jnp.zeros((288, 256), F32)
        for n in range(0, count, step):
            lefts, rights = [], []
            rows = codes_ref[at8(eight), n : n + step]
            for mm in range(4):
                row = rows[quad * 4 + mm : quad * 4 + mm + 1]
                low = jnp.broadcast_to((row & 63).astype(F32), (16, step)).astype(BF16)
                top = jnp.broadcast_to((row >> 6).astype(F32), (16, step)).astype(BF16)
                value = rotated_ref[eight * 8 + quad * 4 + mm, :, n : n + step]
                high = value.astype(BF16).astype(F32)
                both = jnp.concatenate([high, value - high], axis=0).astype(BF16)
                for t in range(4):
                    lefts.append(jnp.where(top == tops[t], both, zero))
                    rights.append(jnp.where(low == marks[t], one, zero))
            tall = (rows >> 6).astype(F32)
            tall = jnp.concatenate([tall, tall], axis=0).astype(BF16)
            for t in range(2):
                pattern = jnp.where(rows16 < 8, 2.0 * t, 2.0 * t + 1.0).astype(BF16)
                lefts.append(jnp.where(tall == pattern, one, zero))
            total += mxu(jnp.concatenate(lefts, axis=0), jnp.concatenate(rights, axis=0), NT)
        found = []
        for mm in range(4):
            columns = slice((mm // 2) * 128, (mm // 2) * 128 + 128)
            slab = total[mm * 64 : mm * 64 + 64, columns]
            parts = [slab[t * 16 : t * 16 + 8] + slab[t * 16 + 8 : t * 16 + 16] for t in range(4)]
            tally = [total[256 + t * 8 : 264 + t * 8, columns] for t in range(4)]
            halves = [pick(parts[2 * h], parts[2 * h + 1], mm) for h in range(2)]
            r = quad * 4 + mm
            ticks = [pick(tally[2 * h], tally[2 * h + 1], mm)[r : r + 1] for h in range(2)]
            ticks = jnp.concatenate(ticks + [jnp.zeros((6, 128), F32)], axis=0)
            found.append(jnp.concatenate(halves + [ticks], axis=1))
        for h in range(2):
            even, odd = found[2 * h], found[2 * h + 1]
            q = eight * 4 + quad * 2 + h
            keep_ref[q] = jnp.where(core == 0, even, odd)
            give_ref[q] = jnp.where(core == 0, odd, even)

    def eight_rows(eight, carry):
        group(eight, 0)
        group(eight, 1)
        return carry

    lax.fori_loop(0, M // 8, eight_rows, 0)


def code_sums(place, points, pieces, codes):
    count = points.shape[0]
    half = jax.ShapeDtypeStruct((M // 2, SUB, PAYLOAD), F32)
    return pl.pallas_call(
        sums_kernel,
        out_shape=(half, half),
        in_specs=[SMEM] + [VMEM] * 6,
        out_specs=(VMEM, VMEM),
        scratch_shapes=[
            pltpu.VMEM((M, count), jnp.int32),
            pltpu.VMEM((256, D), F32),
            pltpu.VMEM((M, SUB, count), F32),
            pltpu.VMEM((count, 256), BF16),
            pltpu.VMEM((count, 256), BF16),
        ],
        compiler_params=PARAMS,
        name="code_sums",
    )(place, points, pieces, *codes)


def cross_kernel(
    place_ref, pts_ref, mine_ref, other_ref, c0, c1, c2, c3,
    keep_ref, give_ref, codes_ref, tab_ref, ah0_ref, al0_ref, ah1_ref, al1_ref, ph_ref, pl_ref, acc_ref,
):
    count = pts_ref.shape[0]
    y, core = place_ref[0], place_ref[1]
    place_codes(codes_ref, y, c0, c1, c2, c3)
    tab_ref[core] = mine_ref[...]
    tab_ref[1 - core] = other_ref[...]
    ph, plo = split(pts_ref[...])
    ph_ref[...] = ph
    pl_ref[...] = plo
    wide = 1024
    quarter = count // 4

    def look_up(block, eight, ah_ref, al_ref):
        for n in range(0, count, wide):
            rows = codes_ref[at8(block * 4 + eight), n : n + wide]
            for two in range(4):
                both = []
                for mm in range(2):
                    index = jnp.broadcast_to(rows[two * 2 + mm : two * 2 + mm + 1], (SUB, wide))
                    table = tab_ref[mm, block * 16 + eight * 4 + two]
                    found = []
                    for k in range(0, wide, 128):
                        here = index[:, k : k + 128]
                        inner = here & 127
                        first = jnp.take_along_axis(
                            table[:, :128], inner, axis=1, mode="promise_in_bounds"
                        )
                        second = jnp.take_along_axis(
                            table[:, 128:], inner, axis=1, mode="promise_in_bounds"
                        )
                        found.append(jnp.where(here < 128, first, second))
                    both.append(jnp.concatenate(found, axis=1))
                high, low = split(jnp.concatenate(both, axis=0))
                place = pl.ds(pl.multiple_of(eight * 64 + two * 16, 16), 16)
                ah_ref[place, n : n + wide] = high
                al_ref[place, n : n + wide] = low

    slots = ((ah0_ref, al0_ref), (ah1_ref, al1_ref))
    for stage in range(5):

        def part(e, carry, stage=stage):
            if stage > 0:
                high_ref, low_ref = slots[(stage - 1) % 2]
                here = pl.ds(pl.multiple_of(e * quarter, 128), quarter)
                more = dot3(high_ref[:, here], low_ref[:, here], ph_ref[here], pl_ref[here], NN)
            if stage < 4:
                look_up(stage, e, *slots[stage % 2])
            if stage > 0:
                acc_ref[...] = more + jnp.where(e == 0, jnp.zeros_like(more), acc_ref[...])
            return carry

        if stage == 1:
            acc_ref[...] = jnp.zeros_like(acc_ref)
        lax.fori_loop(0, 4, part, 0)
        if stage > 0:
            for h in range(4):
                even = acc_ref[h * 64 : h * 64 + 32]
                odd = acc_ref[h * 64 + 32 : h * 64 + 64]
                keep_ref[(stage - 1) * 4 + h] = jnp.where(core == 0, even, odd)
                give_ref[(stage - 1) * 4 + h] = jnp.where(core == 0, odd, even)


def cross_part(place, points, mine, other, codes):
    count = points.shape[0]
    half = jax.ShapeDtypeStruct((16, 32, 256), F32)
    return pl.pallas_call(
        cross_kernel,
        out_shape=(half, half),
        in_specs=[SMEM] + [VMEM] * 7,
        out_specs=(VMEM, VMEM),
        scratch_shapes=[
            pltpu.VMEM((M, count), jnp.int32),
            pltpu.VMEM((2, M // 2, SUB, K), F32),
            pltpu.VMEM((256, count), BF16),
            pltpu.VMEM((256, count), BF16),
            pltpu.VMEM((256, count), BF16),
            pltpu.VMEM((256, count), BF16),
            pltpu.VMEM((count, 256), BF16),
            pltpu.VMEM((count, 256), BF16),
            pltpu.VMEM((256, 256), F32),
        ],
        compiler_params=PARAMS,
        name="cross_part",
    )(place, points, mine, other, *codes)


def iterate_kernel(place_ref, mine_ref, other_ref, out_ref, now_ref, hl_ref, gh_ref, gl_ref, tail_ref, turned_ref):
    y, core, column = place_ref[0], place_ref[1], place_ref[2]
    total = jnp.zeros((1, 256), F32)
    for half, source in enumerate((mine_ref, other_ref)):
        for block in range(4):
            part = source[block * 16 : block * 16 + 16].reshape(512, 256)
            total += jnp.sum(part * part, axis=0, keepdims=True)
    scale = 1.7 / jnp.sqrt(jnp.sum(total, axis=1, keepdims=True) + 1e-06)
    for half, source in enumerate((mine_ref, other_ref)):
        for block in range(4):
            rows, columns = slice(half * 512, half * 512 + 512), slice(block * 256, block * 256 + 256)
            part = source[block * 16 : block * 16 + 16].reshape(512, 256) * scale
            now_ref[rows, columns] = part
            high, low = split(part)
            hl_ref[0, 0, rows, columns] = high
            hl_ref[0, 1, rows, columns] = low

    def step(k, carry):
        old, new = lax.rem(k, 2), 1 - lax.rem(k, 2)
        high_ref, low_ref = hl_ref.at[old, 0], hl_ref.at[old, 1]
        for j in range(4):
            strip, below = slice(j * 256, j * 256 + 256), slice(j * 256, D)
            gram = dot3(high_ref[below], low_ref[below], high_ref[strip], low_ref[strip], NT)
            high, low = split(gram)
            gh_ref[below, strip] = high
            gl_ref[below, strip] = low
            if j < 3:
                high, low = split(gram[256:].T)
                gh_ref[strip, j * 256 + 256 : D] = high
                gl_ref[strip, j * 256 + 256 : D] = low
        for j in range(4):
            strip = slice(j * 256, j * 256 + 256)
            moved = dot3(gh_ref[...], gl_ref[...], high_ref[:, strip], low_ref[:, strip], NN)
            value = 1.5 * now_ref[:, strip] - 0.5 * moved
            now_ref[:, strip] = value
            high, low = split(value)
            hl_ref[new, 0, :, strip] = high
            hl_ref[new, 1, :, strip] = low
        return carry

    lax.fori_loop(0, NS_ITERS - 1, step, 0)
    last = (NS_ITERS - 1) % 2
    high_ref, low_ref = hl_ref.at[last, 0], hl_ref.at[last, 1]
    columns = pl.ds(pl.multiple_of(column // 4 * 128, 128), 128)
    now = []
    for z in range(4):
        for c in range(2):
            half = lax.rem(c + core, 2)
            rows = pl.ds(pl.multiple_of(half * 512 + y * 128 + z * 32, 32), 32)
            here = slice(z * 64 + c * 32, z * 64 + c * 32 + 32)
            tail_ref[0, here] = high_ref[rows]
            tail_ref[1, here] = low_ref[rows]
            now.append(now_ref[rows, columns])
    gram = dot3(tail_ref[0], tail_ref[1], high_ref[...], low_ref[...], NT)
    high, low = split(gram)
    moved = dot3(high, low, high_ref[:, columns], low_ref[:, columns], NN)
    turned_ref[...] = ((1.5 * jnp.concatenate(now, axis=0) - 0.5 * moved) * D**0.5).T
    out_ref[...] = turned_ref[pl.ds(pl.multiple_of(lax.rem(column, 4) * 32, 32), 32), :]


def newton_schulz(place, mine, other):
    return pl.pallas_call(
        iterate_kernel,
        out_shape=jax.ShapeDtypeStruct((32, 256), F32),
        in_specs=[SMEM, VMEM, VMEM],
        out_specs=VMEM,
        scratch_shapes=[
            pltpu.VMEM((D, D), F32),
            pltpu.VMEM((2, 2, D, D), BF16),
            pltpu.VMEM((D, D), BF16),
            pltpu.VMEM((D, D), BF16),
            pltpu.VMEM((2, 256, D), BF16),
            pltpu.VMEM((128, 256), F32),
        ],
        compiler_params=PARAMS,
        name="newton_schulz",
    )(place, mine, other)


def shards(points, codes, rotation):
    y, core = lax.axis_index("y"), lax.axis_index("core")
    own_row = lax.axis_index(ROWS)
    place = jnp.stack([y, core, own_row]).astype(jnp.int32)
    all_codes = [codes] + [
        lax.ppermute(codes, "y", [(s, (s + i) % 4) for s in range(4)]) for i in (1, 2, 3)
    ]
    swapped = lax.ppermute(
        rotation, ("x", "y"), [(a * 4 + b, b * 4 + a) for a in range(4) for b in range(4)]
    )
    pieces = spread_to(jnp.stack([swapped, swap_core(swapped)]), ("x", "z"), 16)
    keep, give = code_sums(place, points, pieces, all_codes)

    sums = keep + swap_core(give)
    sums = jnp.sum(lax.all_to_all(sums, CHIPS, 0, 0, tiled=True), axis=0)
    counts = 0.25 * sums[:2, K:].reshape(1, K)
    centers = spread_to(sums[:, :K] / counts, CHIPS, 64)
    others = swap_core(centers)

    keep, give = cross_part(place, points, centers, others, all_codes)
    block = keep + swap_core(give)
    block = jnp.sum(lax.all_to_all(block, ("x", "z"), 0, 0, tiled=True), axis=0)
    whole = spread_to(block, CHIPS, 64)
    ours = lax.dynamic_slice_in_dim(centers, y * 16, 16, axis=0)
    theirs = lax.dynamic_slice_in_dim(others, y * 16, 16, axis=0)
    first, second = jnp.where(core == 0, ours, theirs), jnp.where(core == 0, theirs, ours)
    centroids = jnp.stack([first, second], axis=1).transpose(0, 1, 3, 2).reshape(32, K * SUB)
    whole, centroids = lax.optimization_barrier((whole, centroids))
    rotated = newton_schulz(place, whole, swap_core(whole))
    return (rotated, centroids)


def solution(mesh):
    grid = Mesh(mesh.devices.reshape(4, 4, 2, 4), ("x", "z", "core", "y"))
    in_specs = (P(ROWS, "y"), P("y", ROWS), P(ROWS, "y"))
    out_specs = (P(ROWS, "y"), P("y", None))
    return jax.shard_map(shards, mesh=grid, in_specs=in_specs, out_specs=out_specs, check_vma=False)
```

```python
import jax
import jax.numpy as jnp
from jax import lax
from jax.experimental import pallas as pl
from jax.experimental.pallas import tpu as pltpu
from jax.sharding import Mesh, PartitionSpec as P

D = 1024
M = 128
K = 256
NS_ITERS = 6
SUB = 8
ROWS = ("x", "z", "core")
CHIPS = ("y", "x", "z")
BF16 = jnp.bfloat16
F32 = jnp.float32
NN = (((1,), (0,)), ((), ()))
NT = (((1,), (1,)), ((), ()))
VMEM = pl.BlockSpec(memory_space=pltpu.VMEM)
SMEM = pl.BlockSpec(memory_space=pltpu.SMEM)
PARAMS = pltpu.CompilerParams(vmem_limit_bytes=56 * 1024 * 1024)
PAYLOAD = K + 128


def split(value):
    high = value.astype(BF16)
    return high, (value - high.astype(F32)).astype(BF16)


def mxu(left, right, dims):
    return lax.dot_general(left, right, dims, preferred_element_type=F32)


def dot3(left_high, left_low, right_high, right_low, dims):
    return (
        mxu(left_high, right_high, dims)
        + mxu(left_high, right_low, dims)
        + mxu(left_low, right_high, dims)
    )


def spread_to(value, axes, count):
    copies = jnp.broadcast_to(value[None], (count,) + value.shape)
    return lax.all_to_all(copies, axes, 0, 0, tiled=True)


def swap_core(value):
    return lax.ppermute(value, "core", [(0, 1), (1, 0)])


def at8(index):
    return pl.ds(pl.multiple_of(index * 8, 8), 8)


def place_codes(where, y, c0, c1, c2, c3):
    for i, codes_ref in enumerate((c0, c1, c2, c3)):
        block = lax.rem(y + 4 - i, 4)
        where[pl.ds(pl.multiple_of(block * 32, 32), 32), :] = codes_ref[...]


def sums_kernel(
    place_ref, pts_ref, pieces_ref, c0, c1, c2, c3,
    keep_ref, give_ref, codes_ref, panel_ref, rotated_ref, ph_ref, pl_ref,
):
    count = pts_ref.shape[0]
    y, core = place_ref[0], place_ref[1]
    place_codes(codes_ref, y, c0, c1, c2, c3)
    ph, plo = split(pts_ref[...])
    ph_ref[...] = ph
    pl_ref[...] = plo
    for a in range(4):
        for z in range(4):
            columns = slice(a * 256, a * 256 + 256)
            first = pl.multiple_of(z * 64 + core * 32, 32)
            second = pl.multiple_of(z * 64 + (1 - core) * 32, 32)
            panel_ref[pl.ds(first, 32), columns] = pieces_ref[a * 4 + z, 0]
            panel_ref[pl.ds(second, 32), columns] = pieces_ref[a * 4 + z, 1]

    def rotate(j, carry):
        panel = panel_ref[:, pl.ds(pl.multiple_of(j * 256, 256), 256)].T
        rh, rl = split(panel)
        part = dot3(rh, rl, ph_ref[...], pl_ref[...], NT)
        rotated_ref[pl.ds(j * 32, 32)] = part.reshape(32, SUB, count)
        return carry

    lax.fori_loop(0, D // 256, rotate, 0)

    step = 512
    rows16 = lax.broadcasted_iota(jnp.int32, (16, step), 0).astype(F32)
    marks = [(rows16 + 16.0 * t).astype(BF16) for t in range(4)]
    tops = [jnp.full((16, step), t, BF16) for t in range(4)]
    one = jnp.ones((16, step), BF16)
    zero = jnp.zeros((16, step), BF16)
    lane = lax.broadcasted_iota(jnp.int32, (SUB, 128), 1)

    def pick(even, odd, mm):
        if mm % 2 == 0:
            odd = pltpu.roll(odd, 64, axis=1)
        else:
            even = pltpu.roll(even, 64, axis=1)
        return jnp.where(lane < 64, even, odd)

    def group(eight, quad):
        total = jnp.zeros((288, 256), F32)
        for n in range(0, count, step):
            lefts, rights = [], []
            rows = codes_ref[at8(eight), n : n + step]
            for mm in range(4):
                row = rows[quad * 4 + mm : quad * 4 + mm + 1]
                low = jnp.broadcast_to((row & 63).astype(F32), (16, step)).astype(BF16)
                top = jnp.broadcast_to((row >> 6).astype(F32), (16, step)).astype(BF16)
                value = rotated_ref[eight * 8 + quad * 4 + mm, :, n : n + step]
                high = value.astype(BF16).astype(F32)
                both = jnp.concatenate([high, value - high], axis=0).astype(BF16)
                for t in range(4):
                    lefts.append(jnp.where(top == tops[t], both, zero))
                    rights.append(jnp.where(low == marks[t], one, zero))
            tall = (rows >> 6).astype(F32)
            tall = jnp.concatenate([tall, tall], axis=0).astype(BF16)
            for t in range(2):
                pattern = jnp.where(rows16 < 8, 2.0 * t, 2.0 * t + 1.0).astype(BF16)
                lefts.append(jnp.where(tall == pattern, one, zero))
            total += mxu(jnp.concatenate(lefts, axis=0), jnp.concatenate(rights, axis=0), NT)
        found = []
        for mm in range(4):
            columns = slice((mm // 2) * 128, (mm // 2) * 128 + 128)
            slab = total[mm * 64 : mm * 64 + 64, columns]
            parts = [slab[t * 16 : t * 16 + 8] + slab[t * 16 + 8 : t * 16 + 16] for t in range(4)]
            tally = [total[256 + t * 8 : 264 + t * 8, columns] for t in range(4)]
            halves = [pick(parts[2 * h], parts[2 * h + 1], mm) for h in range(2)]
            r = quad * 4 + mm
            ticks = [pick(tally[2 * h], tally[2 * h + 1], mm)[r : r + 1] for h in range(2)]
            ticks = jnp.concatenate(ticks + [jnp.zeros((6, 128), F32)], axis=0)
            found.append(jnp.concatenate(halves + [ticks], axis=1))
        for h in range(2):
            even, odd = found[2 * h], found[2 * h + 1]
            q = eight * 4 + quad * 2 + h
            keep_ref[q] = jnp.where(core == 0, even, odd)
            give_ref[q] = jnp.where(core == 0, odd, even)

    def eight_rows(eight, carry):
        group(eight, 0)
        group(eight, 1)
        return carry

    lax.fori_loop(0, M // 8, eight_rows, 0)


def code_sums(place, points, pieces, codes):
    count = points.shape[0]
    half = jax.ShapeDtypeStruct((M // 2, SUB, PAYLOAD), F32)
    return pl.pallas_call(
        sums_kernel,
        out_shape=(half, half),
        in_specs=[SMEM] + [VMEM] * 6,
        out_specs=(VMEM, VMEM),
        scratch_shapes=[
            pltpu.VMEM((M, count), jnp.int32),
            pltpu.VMEM((256, D), F32),
            pltpu.VMEM((M, SUB, count), F32),
            pltpu.VMEM((count, 256), BF16),
            pltpu.VMEM((count, 256), BF16),
        ],
        compiler_params=PARAMS,
        name="code_sums",
    )(place, points, pieces, *codes)


def cross_kernel(
    place_ref, pts_ref, mine_ref, other_ref, c0, c1, c2, c3,
    keep_ref, give_ref, codes_ref, tab_ref, ah0_ref, al0_ref, ah1_ref, al1_ref, ph_ref, pl_ref, acc_ref,
):
    count = pts_ref.shape[0]
    y, core = place_ref[0], place_ref[1]
    place_codes(codes_ref, y, c0, c1, c2, c3)
    tab_ref[core] = mine_ref[...]
    tab_ref[1 - core] = other_ref[...]
    ph, plo = split(pts_ref[...])
    ph_ref[...] = ph
    pl_ref[...] = plo
    wide = 1024
    quarter = count // 4

    def look_up(block, eight, ah_ref, al_ref):
        for n in range(0, count, wide):
            rows = codes_ref[at8(block * 4 + eight), n : n + wide]
            for two in range(4):
                both = []
                for mm in range(2):
                    index = jnp.broadcast_to(rows[two * 2 + mm : two * 2 + mm + 1], (SUB, wide))
                    table = tab_ref[mm, block * 16 + eight * 4 + two]
                    found = []
                    for k in range(0, wide, 128):
                        here = index[:, k : k + 128]
                        inner = here & 127
                        first = jnp.take_along_axis(
                            table[:, :128], inner, axis=1, mode="promise_in_bounds"
                        )
                        second = jnp.take_along_axis(
                            table[:, 128:], inner, axis=1, mode="promise_in_bounds"
                        )
                        found.append(jnp.where(here < 128, first, second))
                    both.append(jnp.concatenate(found, axis=1))
                high, low = split(jnp.concatenate(both, axis=0))
                place = pl.ds(pl.multiple_of(eight * 64 + two * 16, 16), 16)
                ah_ref[place, n : n + wide] = high
                al_ref[place, n : n + wide] = low

    slots = ((ah0_ref, al0_ref), (ah1_ref, al1_ref))
    for stage in range(5):

        def part(e, carry, stage=stage):
            if stage > 0:
                high_ref, low_ref = slots[(stage - 1) % 2]
                here = pl.ds(pl.multiple_of(e * quarter, 128), quarter)
                more = dot3(high_ref[:, here], low_ref[:, here], ph_ref[here], pl_ref[here], NN)
            if stage < 4:
                look_up(stage, e, *slots[stage % 2])
            if stage > 0:
                acc_ref[...] = more + jnp.where(e == 0, jnp.zeros_like(more), acc_ref[...])
            return carry

        if stage == 1:
            acc_ref[...] = jnp.zeros_like(acc_ref)
        lax.fori_loop(0, 4, part, 0)
        if stage > 0:
            for h in range(4):
                even = acc_ref[h * 64 : h * 64 + 32]
                odd = acc_ref[h * 64 + 32 : h * 64 + 64]
                keep_ref[(stage - 1) * 4 + h] = jnp.where(core == 0, even, odd)
                give_ref[(stage - 1) * 4 + h] = jnp.where(core == 0, odd, even)


def cross_part(place, points, mine, other, codes):
    count = points.shape[0]
    half = jax.ShapeDtypeStruct((16, 32, 256), F32)
    return pl.pallas_call(
        cross_kernel,
        out_shape=(half, half),
        in_specs=[SMEM] + [VMEM] * 7,
        out_specs=(VMEM, VMEM),
        scratch_shapes=[
            pltpu.VMEM((M, count), jnp.int32),
            pltpu.VMEM((2, M // 2, SUB, K), F32),
            pltpu.VMEM((256, count), BF16),
            pltpu.VMEM((256, count), BF16),
            pltpu.VMEM((256, count), BF16),
            pltpu.VMEM((256, count), BF16),
            pltpu.VMEM((count, 256), BF16),
            pltpu.VMEM((count, 256), BF16),
            pltpu.VMEM((256, 256), F32),
        ],
        compiler_params=PARAMS,
        name="cross_part",
    )(place, points, mine, other, *codes)


def iterate_kernel(place_ref, mine_ref, other_ref, out_ref, now_ref, hl_ref, gh_ref, gl_ref, tail_ref, turned_ref):
    y, core, column = place_ref[0], place_ref[1], place_ref[2]
    total = jnp.zeros((1, 256), F32)
    for half, source in enumerate((mine_ref, other_ref)):
        for block in range(4):
            part = source[block * 16 : block * 16 + 16].reshape(512, 256)
            total += jnp.sum(part * part, axis=0, keepdims=True)
    scale = 1.7 / jnp.sqrt(jnp.sum(total, axis=1, keepdims=True) + 1e-06)
    for half, source in enumerate((mine_ref, other_ref)):
        for block in range(4):
            rows, columns = slice(half * 512, half * 512 + 512), slice(block * 256, block * 256 + 256)
            part = source[block * 16 : block * 16 + 16].reshape(512, 256) * scale
            now_ref[rows, columns] = part
            high, low = split(part)
            hl_ref[0, 0, rows, columns] = high
            hl_ref[0, 1, rows, columns] = low

    def step(k, carry):
        old, new = lax.rem(k, 2), 1 - lax.rem(k, 2)
        high_ref, low_ref = hl_ref.at[old, 0], hl_ref.at[old, 1]
        for j in range(4):
            strip, below = slice(j * 256, j * 256 + 256), slice(j * 256, D)
            gram = dot3(high_ref[below], low_ref[below], high_ref[strip], low_ref[strip], NT)
            high, low = split(gram)
            gh_ref[below, strip] = high
            gl_ref[below, strip] = low
            if j < 3:
                high, low = split(gram[256:].T)
                gh_ref[strip, j * 256 + 256 : D] = high
                gl_ref[strip, j * 256 + 256 : D] = low
        for j in range(4):
            strip = slice(j * 256, j * 256 + 256)
            moved = dot3(gh_ref[...], gl_ref[...], high_ref[:, strip], low_ref[:, strip], NN)
            value = 1.5 * now_ref[:, strip] - 0.5 * moved
            now_ref[:, strip] = value
            high, low = split(value)
            hl_ref[new, 0, :, strip] = high
            hl_ref[new, 1, :, strip] = low
        return carry

    lax.fori_loop(0, NS_ITERS - 1, step, 0)
    last = (NS_ITERS - 1) % 2
    high_ref, low_ref = hl_ref.at[last, 0], hl_ref.at[last, 1]
    columns = pl.ds(pl.multiple_of(column // 4 * 128, 128), 128)
    now = []
    for z in range(4):
        for c in range(2):
            half = lax.rem(c + core, 2)
            rows = pl.ds(pl.multiple_of(half * 512 + y * 128 + z * 32, 32), 32)
            here = slice(z * 64 + c * 32, z * 64 + c * 32 + 32)
            tail_ref[0, here] = high_ref[rows]
            tail_ref[1, here] = low_ref[rows]
            now.append(now_ref[rows, columns])
    gram = dot3(tail_ref[0], tail_ref[1], high_ref[...], low_ref[...], NT)
    high, low = split(gram)
    moved = dot3(high, low, high_ref[:, columns], low_ref[:, columns], NN)
    turned_ref[...] = ((1.5 * jnp.concatenate(now, axis=0) - 0.5 * moved) * D**0.5).T
    out_ref[...] = turned_ref[pl.ds(pl.multiple_of(lax.rem(column, 4) * 32, 32), 32), :]


def newton_schulz(place, mine, other):
    return pl.pallas_call(
        iterate_kernel,
        out_shape=jax.ShapeDtypeStruct((32, 256), F32),
        in_specs=[SMEM, VMEM, VMEM],
        out_specs=VMEM,
        scratch_shapes=[
            pltpu.VMEM((D, D), F32),
            pltpu.VMEM((2, 2, D, D), BF16),
            pltpu.VMEM((D, D), BF16),
            pltpu.VMEM((D, D), BF16),
            pltpu.VMEM((2, 256, D), BF16),
            pltpu.VMEM((128, 256), F32),
        ],
        compiler_params=PARAMS,
        name="newton_schulz",
    )(place, mine, other)


def shards(points, codes, rotation):
    y, core = lax.axis_index("y"), lax.axis_index("core")
    own_row = lax.axis_index(ROWS)
    place = jnp.stack([y, core, own_row]).astype(jnp.int32)
    one = lax.ppermute(codes, "y", [(s, (s + 1) % 4) for s in range(4)])
    three = lax.ppermute(codes, "y", [(s, (s + 3) % 4) for s in range(4)])
    swapped = lax.ppermute(
        rotation, ("x", "y"), [(a * 4 + b, b * 4 + a) for a in range(4) for b in range(4)]
    )
    pieces = jnp.stack([swapped, swap_core(swapped)])
    pieces, one, three = lax.optimization_barrier((pieces, one, three))
    pieces = spread_to(pieces, ("x", "z"), 16)
    two = lax.ppermute(one, "y", [(s, (s + 1) % 4) for s in range(4)])
    all_codes = [codes, one, two, three]
    keep, give = code_sums(place, points, pieces, all_codes)

    sums = keep + swap_core(give)
    sums = jnp.sum(lax.all_to_all(sums, CHIPS, 0, 0, tiled=True), axis=0)
    counts = 0.25 * sums[:2, K:].reshape(1, K)
    centers = spread_to(sums[:, :K] / counts, CHIPS, 64)
    others = swap_core(centers)

    keep, give = cross_part(place, points, centers, others, all_codes)
    block = keep + swap_core(give)
    block = jnp.sum(lax.all_to_all(block, ("x", "z"), 0, 0, tiled=True), axis=0)
    whole = spread_to(block, CHIPS, 64)
    ours = lax.dynamic_slice_in_dim(centers, y * 16, 16, axis=0)
    theirs = lax.dynamic_slice_in_dim(others, y * 16, 16, axis=0)
    first, second = jnp.where(core == 0, ours, theirs), jnp.where(core == 0, theirs, ours)
    centroids = jnp.stack([first, second], axis=1).transpose(0, 1, 3, 2).reshape(32, K * SUB)
    whole, centroids = lax.optimization_barrier((whole, centroids))
    rotated = newton_schulz(place, whole, swap_core(whole))
    return (rotated, centroids)


def solution(mesh):
    grid = Mesh(mesh.devices.reshape(4, 4, 2, 4), ("x", "z", "core", "y"))
    in_specs = (P(ROWS, "y"), P("y", ROWS), P(ROWS, "y"))
    out_specs = (P(ROWS, "y"), P("y", None))
    return jax.shard_map(shards, mesh=grid, in_specs=in_specs, out_specs=out_specs, check_vma=False)
```

```python
import jax
import jax.numpy as jnp
from jax import lax
from jax.experimental import pallas as pl
from jax.experimental.pallas import tpu as pltpu
from jax.sharding import Mesh, PartitionSpec as P

D = 1024
M = 128
K = 256
NS_ITERS = 6
SUB = 8
ROWS = ("x", "z", "core")
CHIPS = ("y", "x", "z")
BF16 = jnp.bfloat16
F32 = jnp.float32
NN = (((1,), (0,)), ((), ()))
NT = (((1,), (1,)), ((), ()))
VMEM = pl.BlockSpec(memory_space=pltpu.VMEM)
SMEM = pl.BlockSpec(memory_space=pltpu.SMEM)


def grant(mebibytes):
    return pltpu.CompilerParams(vmem_limit_bytes=mebibytes * 1024 * 1024)


PAYLOAD = K + 128


def split(value):
    high = value.astype(BF16)
    return high, (value - high.astype(F32)).astype(BF16)


def mxu(left, right, dims):
    return lax.dot_general(left, right, dims, preferred_element_type=F32)


def dot3(left_high, left_low, right_high, right_low, dims):
    return (
        mxu(left_high, right_high, dims)
        + mxu(left_high, right_low, dims)
        + mxu(left_low, right_high, dims)
    )


def spread_to(value, axes, count):
    copies = jnp.broadcast_to(value[None], (count,) + value.shape)
    return lax.all_to_all(copies, axes, 0, 0, tiled=True)


def swap_core(value):
    return lax.ppermute(value, "core", [(0, 1), (1, 0)])


def at8(index):
    return pl.ds(pl.multiple_of(index * 8, 8), 8)


def place_codes(where, y, c0, c1, c2, c3):
    for i, codes_ref in enumerate((c0, c1, c2, c3)):
        block = lax.rem(y + 4 - i, 4)
        where[pl.ds(pl.multiple_of(block * 32, 32), 32), :] = codes_ref[...]


def sums_kernel(
    place_ref, pts_ref, pieces_ref, c0, c1, c2, c3,
    keep_ref, give_ref, codes_ref, panel_ref, rotated_ref, ph_ref, pl_ref,
):
    count = pts_ref.shape[0]
    y, core = place_ref[0], place_ref[1]
    place_codes(codes_ref, y, c0, c1, c2, c3)
    ph, plo = split(pts_ref[...])
    ph_ref[...] = ph
    pl_ref[...] = plo
    for a in range(4):
        for z in range(4):
            columns = slice(a * 256, a * 256 + 256)
            first = pl.multiple_of(z * 64 + core * 32, 32)
            second = pl.multiple_of(z * 64 + (1 - core) * 32, 32)
            panel_ref[pl.ds(first, 32), columns] = pieces_ref[a * 4 + z, 0]
            panel_ref[pl.ds(second, 32), columns] = pieces_ref[a * 4 + z, 1]

    def rotate(j, carry):
        panel = panel_ref[:, pl.ds(pl.multiple_of(j * 256, 256), 256)].T
        rh, rl = split(panel)
        part = dot3(rh, rl, ph_ref[...], pl_ref[...], NT)
        rotated_ref[pl.ds(j * 32, 32)] = part.reshape(32, SUB, count)
        return carry

    lax.fori_loop(0, D // 256, rotate, 0)

    step = 512
    rows16 = lax.broadcasted_iota(jnp.int32, (16, step), 0).astype(F32)
    marks = [(rows16 + 16.0 * t).astype(BF16) for t in range(4)]
    tops = [jnp.full((16, step), t, BF16) for t in range(4)]
    one = jnp.ones((16, step), BF16)
    zero = jnp.zeros((16, step), BF16)
    lane = lax.broadcasted_iota(jnp.int32, (SUB, 128), 1)

    def pick(even, odd, mm):
        if mm % 2 == 0:
            odd = pltpu.roll(odd, 64, axis=1)
        else:
            even = pltpu.roll(even, 64, axis=1)
        return jnp.where(lane < 64, even, odd)

    def group(eight, quad):
        total = jnp.zeros((288, 256), F32)
        for n in range(0, count, step):
            lefts, rights = [], []
            rows = codes_ref[at8(eight), n : n + step]
            for mm in range(4):
                row = rows[quad * 4 + mm : quad * 4 + mm + 1]
                low = jnp.broadcast_to((row & 63).astype(F32), (16, step)).astype(BF16)
                top = jnp.broadcast_to((row >> 6).astype(F32), (16, step)).astype(BF16)
                value = rotated_ref[eight * 8 + quad * 4 + mm, :, n : n + step]
                high = value.astype(BF16).astype(F32)
                both = jnp.concatenate([high, value - high], axis=0).astype(BF16)
                for t in range(4):
                    lefts.append(jnp.where(top == tops[t], both, zero))
                    rights.append(jnp.where(low == marks[t], one, zero))
            tall = (rows >> 6).astype(F32)
            tall = jnp.concatenate([tall, tall], axis=0).astype(BF16)
            for t in range(2):
                pattern = jnp.where(rows16 < 8, 2.0 * t, 2.0 * t + 1.0).astype(BF16)
                lefts.append(jnp.where(tall == pattern, one, zero))
            total += mxu(jnp.concatenate(lefts, axis=0), jnp.concatenate(rights, axis=0), NT)
        found = []
        for mm in range(4):
            columns = slice((mm // 2) * 128, (mm // 2) * 128 + 128)
            slab = total[mm * 64 : mm * 64 + 64, columns]
            parts = [slab[t * 16 : t * 16 + 8] + slab[t * 16 + 8 : t * 16 + 16] for t in range(4)]
            tally = [total[256 + t * 8 : 264 + t * 8, columns] for t in range(4)]
            halves = [pick(parts[2 * h], parts[2 * h + 1], mm) for h in range(2)]
            r = quad * 4 + mm
            ticks = [pick(tally[2 * h], tally[2 * h + 1], mm)[r : r + 1] for h in range(2)]
            ticks = jnp.concatenate(ticks + [jnp.zeros((6, 128), F32)], axis=0)
            found.append(jnp.concatenate(halves + [ticks], axis=1))
        for h in range(2):
            even, odd = found[2 * h], found[2 * h + 1]
            q = eight * 4 + quad * 2 + h
            keep_ref[q] = jnp.where(core == 0, even, odd)
            give_ref[q] = jnp.where(core == 0, odd, even)

    def eight_rows(eight, carry):
        group(eight, 0)
        group(eight, 1)
        return carry

    lax.fori_loop(0, M // 8, eight_rows, 0)


def code_sums(place, points, pieces, codes):
    count = points.shape[0]
    half = jax.ShapeDtypeStruct((M // 2, SUB, PAYLOAD), F32)
    return pl.pallas_call(
        sums_kernel,
        out_shape=(half, half),
        in_specs=[SMEM] + [VMEM] * 6,
        out_specs=(VMEM, VMEM),
        scratch_shapes=[
            pltpu.VMEM((M, count), jnp.int32),
            pltpu.VMEM((256, D), F32),
            pltpu.VMEM((M, SUB, count), F32),
            pltpu.VMEM((count, 256), BF16),
            pltpu.VMEM((count, 256), BF16),
        ],
        compiler_params=grant(36),
        name="code_sums",
    )(place, points, pieces, *codes)


def cross_kernel(
    place_ref, pts_ref, mine_ref, other_ref, c0, c1, c2, c3,
    keep_ref, give_ref, codes_ref, tab_ref, ah0_ref, al0_ref, ah1_ref, al1_ref, ph_ref, pl_ref, acc_ref,
):
    count = pts_ref.shape[0]
    y, core = place_ref[0], place_ref[1]
    place_codes(codes_ref, y, c0, c1, c2, c3)
    tab_ref[core] = mine_ref[...]
    tab_ref[1 - core] = other_ref[...]
    ph, plo = split(pts_ref[...])
    ph_ref[...] = ph
    pl_ref[...] = plo
    wide = 1024
    quarter = count // 4

    def look_up(block, eight, ah_ref, al_ref):
        for n in range(0, count, wide):
            rows = codes_ref[at8(block * 4 + eight), n : n + wide]
            for two in range(4):
                both = []
                for mm in range(2):
                    index = jnp.broadcast_to(rows[two * 2 + mm : two * 2 + mm + 1], (SUB, wide))
                    table = tab_ref[mm, block * 16 + eight * 4 + two]
                    found = []
                    for k in range(0, wide, 128):
                        here = index[:, k : k + 128]
                        inner = here & 127
                        first = jnp.take_along_axis(
                            table[:, :128], inner, axis=1, mode="promise_in_bounds"
                        )
                        second = jnp.take_along_axis(
                            table[:, 128:], inner, axis=1, mode="promise_in_bounds"
                        )
                        found.append(jnp.where(here < 128, first, second))
                    both.append(jnp.concatenate(found, axis=1))
                high, low = split(jnp.concatenate(both, axis=0))
                place = pl.ds(pl.multiple_of(eight * 64 + two * 16, 16), 16)
                ah_ref[place, n : n + wide] = high
                al_ref[place, n : n + wide] = low

    slots = ((ah0_ref, al0_ref), (ah1_ref, al1_ref))
    for stage in range(5):

        def part(e, carry, stage=stage):
            if stage > 0:
                high_ref, low_ref = slots[(stage - 1) % 2]
                here = pl.ds(pl.multiple_of(e * quarter, 128), quarter)
                more = dot3(high_ref[:, here], low_ref[:, here], ph_ref[here], pl_ref[here], NN)
            if stage < 4:
                look_up(stage, e, *slots[stage % 2])
            if stage > 0:
                acc_ref[...] = more + jnp.where(e == 0, jnp.zeros_like(more), acc_ref[...])
            return carry

        if stage == 1:
            acc_ref[...] = jnp.zeros_like(acc_ref)
        lax.fori_loop(0, 4, part, 0)
        if stage > 0:
            for h in range(4):
                even = acc_ref[h * 64 : h * 64 + 32]
                odd = acc_ref[h * 64 + 32 : h * 64 + 64]
                keep_ref[(stage - 1) * 4 + h] = jnp.where(core == 0, even, odd)
                give_ref[(stage - 1) * 4 + h] = jnp.where(core == 0, odd, even)


def cross_part(place, points, mine, other, codes):
    count = points.shape[0]
    half = jax.ShapeDtypeStruct((16, 32, 256), F32)
    return pl.pallas_call(
        cross_kernel,
        out_shape=(half, half),
        in_specs=[SMEM] + [VMEM] * 7,
        out_specs=(VMEM, VMEM),
        scratch_shapes=[
            pltpu.VMEM((M, count), jnp.int32),
            pltpu.VMEM((2, M // 2, SUB, K), F32),
            pltpu.VMEM((256, count), BF16),
            pltpu.VMEM((256, count), BF16),
            pltpu.VMEM((256, count), BF16),
            pltpu.VMEM((256, count), BF16),
            pltpu.VMEM((count, 256), BF16),
            pltpu.VMEM((count, 256), BF16),
            pltpu.VMEM((256, 256), F32),
        ],
        compiler_params=grant(28),
        name="cross_part",
    )(place, points, mine, other, *codes)


def iterate_kernel(place_ref, mine_ref, other_ref, out_ref, now_ref, hl_ref, gh_ref, gl_ref, tail_ref, turned_ref):
    y, core, column = place_ref[0], place_ref[1], place_ref[2]
    total = jnp.zeros((1, 256), F32)
    for half, source in enumerate((mine_ref, other_ref)):
        for block in range(4):
            part = source[block * 16 : block * 16 + 16].reshape(512, 256)
            total += jnp.sum(part * part, axis=0, keepdims=True)
    scale = 1.7 / jnp.sqrt(jnp.sum(total, axis=1, keepdims=True) + 1e-06)
    for half, source in enumerate((mine_ref, other_ref)):
        for block in range(4):
            rows, columns = slice(half * 512, half * 512 + 512), slice(block * 256, block * 256 + 256)
            part = source[block * 16 : block * 16 + 16].reshape(512, 256) * scale
            now_ref[rows, columns] = part
            high, low = split(part)
            hl_ref[0, 0, rows, columns] = high
            hl_ref[0, 1, rows, columns] = low

    def step(k, carry):
        old, new = lax.rem(k, 2), 1 - lax.rem(k, 2)
        high_ref, low_ref = hl_ref.at[old, 0], hl_ref.at[old, 1]
        for j in range(4):
            strip, below = slice(j * 256, j * 256 + 256), slice(j * 256, D)
            gram = dot3(high_ref[below], low_ref[below], high_ref[strip], low_ref[strip], NT)
            high, low = split(gram)
            gh_ref[below, strip] = high
            gl_ref[below, strip] = low
            if j < 3:
                high, low = split(gram[256:].T)
                gh_ref[strip, j * 256 + 256 : D] = high
                gl_ref[strip, j * 256 + 256 : D] = low
        for j in range(4):
            strip = slice(j * 256, j * 256 + 256)
            moved = dot3(gh_ref[...], gl_ref[...], high_ref[:, strip], low_ref[:, strip], NN)
            value = 1.5 * now_ref[:, strip] - 0.5 * moved
            now_ref[:, strip] = value
            high, low = split(value)
            hl_ref[new, 0, :, strip] = high
            hl_ref[new, 1, :, strip] = low
        return carry

    lax.fori_loop(0, NS_ITERS - 1, step, 0)
    last = (NS_ITERS - 1) % 2
    high_ref, low_ref = hl_ref.at[last, 0], hl_ref.at[last, 1]
    columns = pl.ds(pl.multiple_of(column // 4 * 128, 128), 128)
    now = []
    for z in range(4):
        for c in range(2):
            half = lax.rem(c + core, 2)
            rows = pl.ds(pl.multiple_of(half * 512 + y * 128 + z * 32, 32), 32)
            here = slice(z * 64 + c * 32, z * 64 + c * 32 + 32)
            tail_ref[0, here] = high_ref[rows]
            tail_ref[1, here] = low_ref[rows]
            now.append(now_ref[rows, columns])
    gram = dot3(tail_ref[0], tail_ref[1], high_ref[...], low_ref[...], NT)
    high, low = split(gram)
    moved = dot3(high, low, high_ref[:, columns], low_ref[:, columns], NN)
    turned_ref[...] = ((1.5 * jnp.concatenate(now, axis=0) - 0.5 * moved) * D**0.5).T
    out_ref[...] = turned_ref[pl.ds(pl.multiple_of(lax.rem(column, 4) * 32, 32), 32), :]


def newton_schulz(place, mine, other):
    return pl.pallas_call(
        iterate_kernel,
        out_shape=jax.ShapeDtypeStruct((32, 256), F32),
        in_specs=[SMEM, VMEM, VMEM],
        out_specs=VMEM,
        scratch_shapes=[
            pltpu.VMEM((D, D), F32),
            pltpu.VMEM((2, 2, D, D), BF16),
            pltpu.VMEM((D, D), BF16),
            pltpu.VMEM((D, D), BF16),
            pltpu.VMEM((2, 256, D), BF16),
            pltpu.VMEM((128, 256), F32),
        ],
        compiler_params=grant(34),
        name="newton_schulz",
    )(place, mine, other)


def shards(points, codes, rotation):
    y, core = lax.axis_index("y"), lax.axis_index("core")
    own_row = lax.axis_index(ROWS)
    place = jnp.stack([y, core, own_row]).astype(jnp.int32)
    one = lax.ppermute(codes, "y", [(s, (s + 1) % 4) for s in range(4)])
    three = lax.ppermute(codes, "y", [(s, (s + 3) % 4) for s in range(4)])
    swapped = lax.ppermute(
        rotation, ("x", "y"), [(a * 4 + b, b * 4 + a) for a in range(4) for b in range(4)]
    )
    pieces = jnp.stack([swapped, swap_core(swapped)])
    pieces = jnp.broadcast_to(pieces[None], (16,) + pieces.shape)
    pieces, one, three = lax.optimization_barrier((pieces, one, three))
    pieces = lax.all_to_all(pieces, ("x", "z"), 0, 0, tiled=True)
    two = lax.ppermute(one, "y", [(s, (s + 1) % 4) for s in range(4)])
    all_codes = [codes, one, two, three]
    keep, give = code_sums(place, points, pieces, all_codes)

    sums = keep + swap_core(give)
    sums = jnp.sum(lax.all_to_all(sums, CHIPS, 0, 0, tiled=True), axis=0)
    counts = 0.25 * sums[:2, K:].reshape(1, K)
    centers = spread_to(sums[:, :K] / counts, CHIPS, 64)
    others = swap_core(centers)

    keep, give = cross_part(place, points, centers, others, all_codes)
    block = keep + swap_core(give)
    block = jnp.sum(lax.all_to_all(block, ("x", "z"), 0, 0, tiled=True), axis=0)
    whole = spread_to(block, CHIPS, 64)
    ours = lax.dynamic_slice_in_dim(centers, y * 16, 16, axis=0)
    theirs = lax.dynamic_slice_in_dim(others, y * 16, 16, axis=0)
    first, second = jnp.where(core == 0, ours, theirs), jnp.where(core == 0, theirs, ours)
    centroids = jnp.stack([first, second], axis=1).transpose(0, 1, 3, 2).reshape(32, K * SUB)
    whole, centroids = lax.optimization_barrier((whole, centroids))
    rotated = newton_schulz(place, whole, swap_core(whole))
    return (rotated, centroids)


def solution(mesh):
    grid = Mesh(mesh.devices.reshape(4, 4, 2, 4), ("x", "z", "core", "y"))
    in_specs = (P(ROWS, "y"), P("y", ROWS), P(ROWS, "y"))
    out_specs = (P(ROWS, "y"), P("y", None))
    return jax.shard_map(shards, mesh=grid, in_specs=in_specs, out_specs=out_specs, check_vma=False)
```

```python
import functools

import jax
import jax.numpy as jnp
from jax import lax
from jax.experimental import pallas as pl
from jax.experimental.pallas import tpu as pltpu
from jax.sharding import Mesh, PartitionSpec as P

D = 1024
M = 128
K = 256
NS_ITERS = 6
SUB = 8
ROWS = ("x", "z", "core")
CHIPS = ("y", "x", "z")
BF16 = jnp.bfloat16
F32 = jnp.float32
NN = (((1,), (0,)), ((), ()))
NT = (((1,), (1,)), ((), ()))
VMEM = pl.BlockSpec(memory_space=pltpu.VMEM)
SMEM = pl.BlockSpec(memory_space=pltpu.SMEM)
ANY = pl.BlockSpec(memory_space=pl.ANY)


def grant(mebibytes):
    return pltpu.CompilerParams(vmem_limit_bytes=mebibytes * 1024 * 1024)


PAYLOAD = K + 128


def split(value):
    high = value.astype(BF16)
    return high, (value - high.astype(F32)).astype(BF16)


def mxu(left, right, dims):
    return lax.dot_general(left, right, dims, preferred_element_type=F32)


def dot3(left_high, left_low, right_high, right_low, dims):
    return (
        mxu(left_high, right_high, dims)
        + mxu(left_high, right_low, dims)
        + mxu(left_low, right_high, dims)
    )


def spread_to(value, axes, count):
    copies = jnp.broadcast_to(value[None], (count,) + value.shape)
    return lax.all_to_all(copies, axes, 0, 0, tiled=True)


def swap_core(value):
    return lax.ppermute(value, "core", [(0, 1), (1, 0)])


def shift(value, by):
    return lax.ppermute(value, "y", [(s, (s + by) % 4) for s in range(4)])


def at8(index):
    return pl.ds(pl.multiple_of(index * 8, 8), 8)


def fetch_codes(y, codes_ref, sources, arrived):
    places = ((0, 0), (1, 0), (1, 1), (2, 0), (2, 1), (3, 0), (3, 1))
    copies = []
    for number, (source, (back, half)) in enumerate(zip(sources, places, strict=True)):
        first = pl.multiple_of(lax.rem(y + 4 - back, 4) * 32 + half * 16, 16)
        target = codes_ref.at[pl.ds(first, source.shape[0]), :]
        copies.append(pltpu.make_async_copy(source, target, arrived.at[number]))
    for copy in copies:
        copy.start()
    return copies


def sums_kernel(
    place_ref, pts_ref, pieces_ref, c0, c1a, c1b, c2a, c2b, c3a, c3b,
    keep_ref, give_ref, codes_ref, ph_ref, pl_ref, panel_ref, rotated_ref, arrived,
):
    count = pts_ref.shape[0]
    y, core = place_ref[0], place_ref[1]
    copies = fetch_codes(y, codes_ref, (c0, c1a, c1b, c2a, c2b, c3a, c3b), arrived)
    ph, plo = split(pts_ref[...])
    ph_ref[...] = ph
    pl_ref[...] = plo
    for a in range(4):
        for part in range(8):
            panel_ref[part * 32 : part * 32 + 32, a * 256 : a * 256 + 256] = pieces_ref[a * 8 + part]

    def rotate(j, carry):
        panel = panel_ref[:, pl.ds(pl.multiple_of(j * 256, 256), 256)].T
        rh, rl = split(panel)
        part = dot3(rh, rl, ph_ref[...], pl_ref[...], NT)
        rotated_ref[pl.ds(j * 32, 32)] = part.reshape(32, SUB, count)
        return carry

    lax.fori_loop(0, D // 256, rotate, 0)
    for copy in copies:
        copy.wait()

    step = 512
    rows16 = lax.broadcasted_iota(jnp.int32, (16, step), 0).astype(F32)
    marks = [(rows16 + 16.0 * t).astype(BF16) for t in range(4)]
    tops = [jnp.full((16, step), t, BF16) for t in range(4)]
    one = jnp.ones((16, step), BF16)
    zero = jnp.zeros((16, step), BF16)
    lane = lax.broadcasted_iota(jnp.int32, (SUB, 128), 1)

    def pick(even, odd, mm):
        if mm % 2 == 0:
            odd = pltpu.roll(odd, 64, axis=1)
        else:
            even = pltpu.roll(even, 64, axis=1)
        return jnp.where(lane < 64, even, odd)

    def group(eight, quad, counted):
        total = jnp.zeros((288 if counted else 256, 256), F32)
        for n in range(0, count, step):
            lefts, rights = [], []
            rows = codes_ref[at8(eight), n : n + step]
            for mm in range(4):
                row = rows[quad * 4 + mm : quad * 4 + mm + 1]
                low = jnp.broadcast_to((row & 63).astype(F32), (16, step)).astype(BF16)
                top = jnp.broadcast_to((row >> 6).astype(F32), (16, step)).astype(BF16)
                value = rotated_ref[eight * 8 + quad * 4 + mm, :, n : n + step]
                high = value.astype(BF16).astype(F32)
                both = jnp.concatenate([high, value - high], axis=0).astype(BF16)
                for t in range(4):
                    lefts.append(jnp.where(top == tops[t], both, zero))
                    rights.append(jnp.where(low == marks[t], one, zero))
            if counted:
                tall = (rows >> 6).astype(F32)
                tall = jnp.concatenate([tall, tall], axis=0).astype(BF16)
                for t in range(2):
                    pattern = jnp.where(rows16 < 8, 2.0 * t, 2.0 * t + 1.0).astype(BF16)
                    lefts.append(jnp.where(tall == pattern, one, zero))
            total += mxu(jnp.concatenate(lefts, axis=0), jnp.concatenate(rights, axis=0), NT)
        found = []
        for mm in range(4):
            columns = slice((mm // 2) * 128, (mm // 2) * 128 + 128)
            slab = total[mm * 64 : mm * 64 + 64, columns]
            parts = [slab[t * 16 : t * 16 + 8] + slab[t * 16 + 8 : t * 16 + 16] for t in range(4)]
            halves = [pick(parts[2 * h], parts[2 * h + 1], mm) for h in range(2)]
            ticks = jnp.zeros((SUB, 128), F32)
            if counted:
                r = quad * 4 + mm
                tally = [total[256 + t * 8 : 264 + t * 8, columns] for t in range(4)]
                ticks = [pick(tally[2 * h], tally[2 * h + 1], mm)[r : r + 1] for h in range(2)]
                ticks = jnp.concatenate(ticks + [jnp.zeros((6, 128), F32)], axis=0)
            found.append(jnp.concatenate(halves + [ticks], axis=1))
        for h in range(2):
            even, odd = found[2 * h], found[2 * h + 1]
            q = eight * 4 + quad * 2 + h
            keep_ref[q] = jnp.where(core == 0, even, odd)
            give_ref[q] = jnp.where(core == 0, odd, even)

    def eight_rows(i, carry, counted):
        eight = lax.rem(y * 4 + i, M // 8)
        group(eight, 0, counted)
        group(eight, 1, counted)
        return carry

    lax.fori_loop(0, 4, functools.partial(eight_rows, counted=True), 0)
    lax.fori_loop(4, M // 8, functools.partial(eight_rows, counted=False), 0)


def code_sums(place, points, pieces, codes):
    count = points.shape[0]
    half = jax.ShapeDtypeStruct((M // 2, SUB, PAYLOAD), F32)
    return pl.pallas_call(
        sums_kernel,
        out_shape=(half, half),
        in_specs=[SMEM, VMEM, VMEM] + [ANY] * len(codes),
        out_specs=(VMEM, VMEM),
        scratch_shapes=[
            pltpu.VMEM((M, count), jnp.int32),
            pltpu.VMEM((count, 256), BF16),
            pltpu.VMEM((count, 256), BF16),
            pltpu.VMEM((256, D), F32),
            pltpu.VMEM((M, SUB, count), F32),
            pltpu.SemaphoreType.DMA((len(codes),)),
        ],
        compiler_params=grant(34),
        name="code_sums",
    )(place, points, pieces, *codes)


def cross_kernel(
    place_ref, pts_ref, mine_ref, other_ref, c0, c1a, c1b, c2a, c2b, c3a, c3b,
    keep_ref, give_ref,
    codes_ref, ph_ref, pl_ref, tab_ref, ah0_ref, al0_ref, ah1_ref, al1_ref, acc_ref, arrived,
):
    count = pts_ref.shape[0]
    y, core = place_ref[0], place_ref[1]
    copies = fetch_codes(y, codes_ref, (c0, c1a, c1b, c2a, c2b, c3a, c3b), arrived)
    tab_ref[core] = mine_ref[...]
    tab_ref[1 - core] = other_ref[...]
    ph, plo = split(pts_ref[...])
    ph_ref[...] = ph
    pl_ref[...] = plo
    for copy in copies:
        copy.wait()
    wide = 1024
    quarter = count // 4

    def look_up(block, eight, ah_ref, al_ref):
        for n in range(0, count, wide):
            rows = codes_ref[at8(block * 4 + eight), n : n + wide]
            for two in range(4):
                both = []
                for mm in range(2):
                    index = jnp.broadcast_to(rows[two * 2 + mm : two * 2 + mm + 1], (SUB, wide))
                    table = tab_ref[mm, block * 16 + eight * 4 + two]
                    found = []
                    for k in range(0, wide, 128):
                        here = index[:, k : k + 128]
                        inner = here & 127
                        first = jnp.take_along_axis(
                            table[:, :128], inner, axis=1, mode="promise_in_bounds"
                        )
                        second = jnp.take_along_axis(
                            table[:, 128:], inner, axis=1, mode="promise_in_bounds"
                        )
                        found.append(jnp.where(here < 128, first, second))
                    both.append(jnp.concatenate(found, axis=1))
                high, low = split(jnp.concatenate(both, axis=0))
                place = pl.ds(pl.multiple_of(eight * 64 + two * 16, 16), 16)
                ah_ref[place, n : n + wide] = high
                al_ref[place, n : n + wide] = low

    slots = ((ah0_ref, al0_ref), (ah1_ref, al1_ref))
    for stage in range(5):

        def part(e, carry, stage=stage):
            if stage > 0:
                high_ref, low_ref = slots[(stage - 1) % 2]
                here = pl.ds(pl.multiple_of(e * quarter, 128), quarter)
                more = dot3(high_ref[:, here], low_ref[:, here], ph_ref[here], pl_ref[here], NN)
            if stage < 4:
                look_up(stage, e, *slots[stage % 2])
            if stage > 0:
                acc_ref[...] = more + jnp.where(e == 0, jnp.zeros_like(more), acc_ref[...])
            return carry

        if stage == 1:
            acc_ref[...] = jnp.zeros_like(acc_ref)
        lax.fori_loop(0, 4, part, 0)
        if stage > 0:
            for h in range(4):
                even = acc_ref[h * 64 : h * 64 + 32]
                odd = acc_ref[h * 64 + 32 : h * 64 + 64]
                keep_ref[(stage - 1) * 4 + h] = jnp.where(core == 0, even, odd)
                give_ref[(stage - 1) * 4 + h] = jnp.where(core == 0, odd, even)


def cross_part(place, points, mine, other, codes):
    count = points.shape[0]
    half = jax.ShapeDtypeStruct((16, 32, 256), F32)
    return pl.pallas_call(
        cross_kernel,
        out_shape=(half, half),
        in_specs=[SMEM] + [VMEM] * 3 + [ANY] * len(codes),
        out_specs=(VMEM, VMEM),
        scratch_shapes=[
            pltpu.VMEM((M, count), jnp.int32),
            pltpu.VMEM((count, 256), BF16),
            pltpu.VMEM((count, 256), BF16),
            pltpu.VMEM((2, M // 2, SUB, K), F32),
            pltpu.VMEM((256, count), BF16),
            pltpu.VMEM((256, count), BF16),
            pltpu.VMEM((256, count), BF16),
            pltpu.VMEM((256, count), BF16),
            pltpu.VMEM((256, 256), F32),
            pltpu.SemaphoreType.DMA((len(codes),)),
        ],
        compiler_params=grant(28),
        name="cross_part",
    )(place, points, mine, other, *codes)


def iterate_kernel(place_ref, mine_ref, other_ref, out_ref, now_ref, hl_ref, gh_ref, gl_ref, tail_ref, turned_ref):
    y, core, column = place_ref[0], place_ref[1], place_ref[2]
    total = jnp.zeros((1, 256), F32)
    for half, source in enumerate((mine_ref, other_ref)):
        for block in range(4):
            part = source[block * 16 : block * 16 + 16].reshape(512, 256)
            total += jnp.sum(part * part, axis=0, keepdims=True)
    scale = 1.7 / jnp.sqrt(jnp.sum(total, axis=1, keepdims=True) + 1e-06)
    for half, source in enumerate((mine_ref, other_ref)):
        for block in range(4):
            rows, columns = slice(half * 512, half * 512 + 512), slice(block * 256, block * 256 + 256)
            part = source[block * 16 : block * 16 + 16].reshape(512, 256) * scale
            now_ref[rows, columns] = part
            high, low = split(part)
            hl_ref[0, 0, rows, columns] = high
            hl_ref[0, 1, rows, columns] = low

    def step(k, carry):
        old, new = lax.rem(k, 2), 1 - lax.rem(k, 2)
        high_ref, low_ref = hl_ref.at[old, 0], hl_ref.at[old, 1]
        for j in range(4):
            strip, below = slice(j * 256, j * 256 + 256), slice(j * 256, D)
            gram = dot3(high_ref[below], low_ref[below], high_ref[strip], low_ref[strip], NT)
            high, low = split(gram)
            gh_ref[below, strip] = high
            gl_ref[below, strip] = low
            if j < 3:
                high, low = split(gram[256:].T)
                gh_ref[strip, j * 256 + 256 : D] = high
                gl_ref[strip, j * 256 + 256 : D] = low
        for j in range(4):
            strip = slice(j * 256, j * 256 + 256)
            moved = dot3(gh_ref[...], gl_ref[...], high_ref[:, strip], low_ref[:, strip], NN)
            value = 1.5 * now_ref[:, strip] - 0.5 * moved
            now_ref[:, strip] = value
            high, low = split(value)
            hl_ref[new, 0, :, strip] = high
            hl_ref[new, 1, :, strip] = low
        return carry

    lax.fori_loop(0, NS_ITERS - 1, step, 0)
    last = (NS_ITERS - 1) % 2
    high_ref, low_ref = hl_ref.at[last, 0], hl_ref.at[last, 1]
    columns = pl.ds(pl.multiple_of(column // 4 * 128, 128), 128)
    now = []
    for z in range(4):
        for c in range(2):
            half = lax.rem(c + core, 2)
            rows = pl.ds(pl.multiple_of(half * 512 + y * 128 + z * 32, 32), 32)
            here = slice(z * 64 + c * 32, z * 64 + c * 32 + 32)
            tail_ref[0, here] = high_ref[rows]
            tail_ref[1, here] = low_ref[rows]
            now.append(now_ref[rows, columns])
    gram = dot3(tail_ref[0], tail_ref[1], high_ref[...], low_ref[...], NT)
    high, low = split(gram)
    moved = dot3(high, low, high_ref[:, columns], low_ref[:, columns], NN)
    turned_ref[...] = ((1.5 * jnp.concatenate(now, axis=0) - 0.5 * moved) * D**0.5).T
    out_ref[...] = turned_ref[pl.ds(pl.multiple_of(lax.rem(column, 4) * 32, 32), 32), :]


def newton_schulz(place, mine, other):
    return pl.pallas_call(
        iterate_kernel,
        out_shape=jax.ShapeDtypeStruct((32, 256), F32),
        in_specs=[SMEM, VMEM, VMEM],
        out_specs=VMEM,
        scratch_shapes=[
            pltpu.VMEM((D, D), F32),
            pltpu.VMEM((2, 2, D, D), BF16),
            pltpu.VMEM((D, D), BF16),
            pltpu.VMEM((D, D), BF16),
            pltpu.VMEM((2, 256, D), BF16),
            pltpu.VMEM((128, 256), F32),
        ],
        compiler_params=grant(34),
        name="newton_schulz",
    )(place, mine, other)


def shards(points, codes, rotation):
    y, core = lax.axis_index("y"), lax.axis_index("core")
    own_row = lax.axis_index(ROWS)
    place = jnp.stack([y, core, own_row]).astype(jnp.int32)
    upper, lower = codes[:16], codes[16:]
    one_a, three_a = shift(upper, 1), shift(upper, 3)
    swapped = lax.ppermute(
        rotation, ("x", "y"), [(a * 4 + b, b * 4 + a) for a in range(4) for b in range(4)]
    )
    swapped, one_a, three_a = lax.optimization_barrier((swapped, one_a, three_a))
    pieces = spread_to(swapped, ROWS, 32)
    one_b, three_b = shift(lower, 1), shift(lower, 3)
    two_a, two_b = shift(one_a, 1), shift(three_b, 3)
    all_codes = [codes, one_a, one_b, two_a, two_b, three_a, three_b]
    keep, give = code_sums(place, points, pieces, all_codes)

    sums = keep + swap_core(give)
    sums = jnp.sum(lax.all_to_all(sums, CHIPS, 0, 0, tiled=True), axis=0)
    counts = sums[:2, K:].reshape(1, K)
    centers = spread_to(sums[:, :K] / counts, CHIPS, 64)
    others = swap_core(centers)

    keep, give = cross_part(place, points, centers, others, all_codes)
    block = keep + swap_core(give)
    block = jnp.sum(lax.all_to_all(block, ("x", "z"), 0, 0, tiled=True), axis=0)
    whole = spread_to(block, CHIPS, 64)
    ours = lax.dynamic_slice_in_dim(centers, y * 16, 16, axis=0)
    theirs = lax.dynamic_slice_in_dim(others, y * 16, 16, axis=0)
    first, second = jnp.where(core == 0, ours, theirs), jnp.where(core == 0, theirs, ours)
    centroids = jnp.stack([first, second], axis=1).transpose(0, 1, 3, 2).reshape(32, K * SUB)
    whole, centroids = lax.optimization_barrier((whole, centroids))
    rotated = newton_schulz(place, whole, swap_core(whole))
    return (rotated, centroids)


def solution(mesh):
    grid = Mesh(mesh.devices.reshape(4, 4, 2, 4), ("x", "z", "core", "y"))
    in_specs = (P(ROWS, "y"), P("y", ROWS), P(ROWS, "y"))
    out_specs = (P(ROWS, "y"), P("y", None))
    return jax.shard_map(shards, mesh=grid, in_specs=in_specs, out_specs=out_specs, check_vma=False)
```

```python
import functools

import jax
import jax.numpy as jnp
from jax import lax
from jax.experimental import pallas as pl
from jax.experimental.pallas import tpu as pltpu
from jax.sharding import Mesh, PartitionSpec as P

D = 1024
M = 128
K = 256
NS_ITERS = 6
SUB = 8
ROWS = ("x", "z", "core")
CHIPS = ("y", "x", "z")
BF16 = jnp.bfloat16
F32 = jnp.float32
NN = (((1,), (0,)), ((), ()))
NT = (((1,), (1,)), ((), ()))
VMEM = pl.BlockSpec(memory_space=pltpu.VMEM)
SMEM = pl.BlockSpec(memory_space=pltpu.SMEM)
ANY = pl.BlockSpec(memory_space=pl.ANY)


def grant(mebibytes):
    return pltpu.CompilerParams(vmem_limit_bytes=mebibytes * 1024 * 1024)


QUARTER = 98304 // 32 // 4
PAYLOAD = K + 128


def split(value):
    high = value.astype(BF16)
    return high, (value - high.astype(F32)).astype(BF16)


def mxu(left, right, dims):
    return lax.dot_general(left, right, dims, preferred_element_type=F32)


def dot3(left_high, left_low, right_high, right_low, dims):
    return (
        mxu(left_high, right_high, dims)
        + mxu(left_high, right_low, dims)
        + mxu(left_low, right_high, dims)
    )


def spread_to(value, axes, count):
    copies = jnp.broadcast_to(value[None], (count,) + value.shape)
    return lax.all_to_all(copies, axes, 0, 0, tiled=True)


def swap_core(value):
    return lax.ppermute(value, "core", [(0, 1), (1, 0)])


def in_hbm(value):
    return pltpu.with_memory_space_constraint(value, pltpu.HBM)


def shift(value, by):
    return lax.ppermute(value, "y", [(s, (s + by) % 4) for s in range(4)])


def at8(index):
    return pl.ds(pl.multiple_of(index * 8, 8), 8)


def fetch_codes(y, codes_ref, sources, arrived):
    copies = []
    for number, source in enumerate(sources):
        first = pl.multiple_of(lax.rem(y + 4 - number, 4) * 32, 32)
        target = codes_ref.at[pl.ds(first, 32), :]
        copies.append(pltpu.make_async_copy(source, target, arrived.at[number]))
    for copy in copies:
        copy.start()
    return copies


def load_points(i, pts_ref, points_ref, arrived):
    chunk = pl.ds(pl.multiple_of(i * QUARTER, QUARTER), QUARTER)
    return pltpu.make_async_copy(pts_ref.at[chunk], points_ref.at[chunk], arrived.at[4 + i])


def split_points(i, points_ref, ph_ref, pl_ref):
    chunk = pl.ds(pl.multiple_of(i * QUARTER, QUARTER), QUARTER)
    high, low = split(points_ref[chunk])
    ph_ref[chunk] = high
    pl_ref[chunk] = low


def sums_kernel(
    place_ref, pts_ref, first_ref, second_ref, c0, c1, c2, c3,
    keep_ref, give_ref, codes_ref, points_ref, ph_ref, pl_ref, panel_ref, rotated_ref, arrived,
):
    count = pts_ref.shape[0]
    y, core = place_ref[0], place_ref[1]
    for i in range(4):
        load_points(i, pts_ref, points_ref, arrived).start()
    copies = fetch_codes(y, codes_ref, (c0, c1, c2, c3), arrived)
    for a in range(4):
        for z in range(4):
            columns = slice(a * 256, a * 256 + 256)
            ours = pl.multiple_of(z * 64 + core * 32, 32)
            theirs = pl.multiple_of(z * 64 + (1 - core) * 32, 32)
            panel_ref[pl.ds(ours, 32), columns] = first_ref[a * 4 + z]
            panel_ref[pl.ds(theirs, 32), columns] = second_ref[a * 4 + z]

    for i in range(4):
        load_points(i, pts_ref, points_ref, arrived).wait()
        split_points(i, points_ref, ph_ref, pl_ref)

    def rotate(j, carry):
        panel = panel_ref[:, pl.ds(pl.multiple_of(j * 256, 256), 256)].T
        rh, rl = split(panel)
        part = dot3(rh, rl, ph_ref[...], pl_ref[...], NT)
        rotated_ref[pl.ds(j * 32, 32)] = part.reshape(32, SUB, count)
        return carry

    lax.fori_loop(0, D // 256, rotate, 0)
    for copy in copies:
        copy.wait()

    step = 512
    rows16 = lax.broadcasted_iota(jnp.int32, (16, step), 0).astype(F32)
    marks = [(rows16 + 16.0 * t).astype(BF16) for t in range(4)]
    tops = [jnp.full((16, step), t, BF16) for t in range(4)]
    one = jnp.ones((16, step), BF16)
    zero = jnp.zeros((16, step), BF16)
    lane = lax.broadcasted_iota(jnp.int32, (SUB, 128), 1)

    def pick(even, odd, mm):
        if mm % 2 == 0:
            odd = pltpu.roll(odd, 64, axis=1)
        else:
            even = pltpu.roll(even, 64, axis=1)
        return jnp.where(lane < 64, even, odd)

    def group(eight, quad, counted):
        total = jnp.zeros((288 if counted else 256, 256), F32)
        for n in range(0, count, step):
            lefts, rights = [], []
            rows = codes_ref[at8(eight), n : n + step]
            for mm in range(4):
                row = rows[quad * 4 + mm : quad * 4 + mm + 1]
                low = jnp.broadcast_to((row & 63).astype(F32), (16, step)).astype(BF16)
                top = jnp.broadcast_to((row >> 6).astype(F32), (16, step)).astype(BF16)
                value = rotated_ref[eight * 8 + quad * 4 + mm, :, n : n + step]
                high = value.astype(BF16).astype(F32)
                both = jnp.concatenate([high, value - high], axis=0).astype(BF16)
                for t in range(4):
                    lefts.append(jnp.where(top == tops[t], both, zero))
                    rights.append(jnp.where(low == marks[t], one, zero))
            if counted:
                tall = (rows >> 6).astype(F32)
                tall = jnp.concatenate([tall, tall], axis=0).astype(BF16)
                for t in range(2):
                    pattern = jnp.where(rows16 < 8, 2.0 * t, 2.0 * t + 1.0).astype(BF16)
                    lefts.append(jnp.where(tall == pattern, one, zero))
            total += mxu(jnp.concatenate(lefts, axis=0), jnp.concatenate(rights, axis=0), NT)
        found = []
        for mm in range(4):
            columns = slice((mm // 2) * 128, (mm // 2) * 128 + 128)
            slab = total[mm * 64 : mm * 64 + 64, columns]
            parts = [slab[t * 16 : t * 16 + 8] + slab[t * 16 + 8 : t * 16 + 16] for t in range(4)]
            halves = [pick(parts[2 * h], parts[2 * h + 1], mm) for h in range(2)]
            ticks = jnp.zeros((SUB, 128), F32)
            if counted:
                r = quad * 4 + mm
                tally = [total[256 + t * 8 : 264 + t * 8, columns] for t in range(4)]
                ticks = [pick(tally[2 * h], tally[2 * h + 1], mm)[r : r + 1] for h in range(2)]
                ticks = jnp.concatenate(ticks + [jnp.zeros((6, 128), F32)], axis=0)
            found.append(jnp.concatenate(halves + [ticks], axis=1))
        for h in range(2):
            even, odd = found[2 * h], found[2 * h + 1]
            q = eight * 4 + quad * 2 + h
            keep_ref[q] = jnp.where(core == 0, even, odd)
            give_ref[q] = jnp.where(core == 0, odd, even)

    def eight_rows(i, carry, counted):
        eight = lax.rem(y * 4 + i, M // 8)
        group(eight, 0, counted)
        group(eight, 1, counted)
        return carry

    lax.fori_loop(0, 4, functools.partial(eight_rows, counted=True), 0)
    lax.fori_loop(4, M // 8, functools.partial(eight_rows, counted=False), 0)


def code_sums(place, points, first, second, codes):
    count = points.shape[0]
    half = jax.ShapeDtypeStruct((M // 2, SUB, PAYLOAD), F32)
    return pl.pallas_call(
        sums_kernel,
        out_shape=(half, half),
        in_specs=[SMEM, ANY, VMEM, VMEM] + [ANY] * len(codes),
        out_specs=(VMEM, VMEM),
        scratch_shapes=[
            pltpu.VMEM((M, count), jnp.int32),
            pltpu.VMEM((count, 256), F32),
            pltpu.VMEM((count, 256), BF16),
            pltpu.VMEM((count, 256), BF16),
            pltpu.VMEM((256, D), F32),
            pltpu.VMEM((M, SUB, count), F32),
            pltpu.SemaphoreType.DMA((8,)),
        ],
        compiler_params=grant(34),
        name="code_sums",
    )(place, points, first, second, *codes)


def cross_kernel(
    place_ref, pts_ref, mine_ref, other_ref, c0, c1, c2, c3,
    keep_ref, give_ref,
    codes_ref, points_ref, ph_ref, pl_ref, tab_ref, ah0_ref, al0_ref, ah1_ref, al1_ref, acc_ref, arrived,
):
    count = pts_ref.shape[0]
    y, core = place_ref[0], place_ref[1]
    copies = fetch_codes(y, codes_ref, (c0, c1, c2, c3), arrived)
    for i in range(4):
        load_points(i, pts_ref, points_ref, arrived).start()
    tab_ref[core] = mine_ref[...]
    tab_ref[1 - core] = other_ref[...]
    for copy in copies:
        copy.wait()
    wide = 1024
    quarter = count // 4

    def look_up(block, eight, ah_ref, al_ref):
        for n in range(0, count, wide):
            rows = codes_ref[at8(block * 4 + eight), n : n + wide]
            for two in range(4):
                both = []
                for mm in range(2):
                    index = jnp.broadcast_to(rows[two * 2 + mm : two * 2 + mm + 1], (SUB, wide))
                    table = tab_ref[mm, block * 16 + eight * 4 + two]
                    found = []
                    for k in range(0, wide, 128):
                        here = index[:, k : k + 128]
                        inner = here & 127
                        first = jnp.take_along_axis(
                            table[:, :128], inner, axis=1, mode="promise_in_bounds"
                        )
                        second = jnp.take_along_axis(
                            table[:, 128:], inner, axis=1, mode="promise_in_bounds"
                        )
                        found.append(jnp.where(here < 128, first, second))
                    both.append(jnp.concatenate(found, axis=1))
                high, low = split(jnp.concatenate(both, axis=0))
                place = pl.ds(pl.multiple_of(eight * 64 + two * 16, 16), 16)
                ah_ref[place, n : n + wide] = high
                al_ref[place, n : n + wide] = low

    slots = ((ah0_ref, al0_ref), (ah1_ref, al1_ref))
    for stage in range(5):

        def part(e, carry, stage=stage):
            if stage > 0:
                high_ref, low_ref = slots[(stage - 1) % 2]
                here = pl.ds(pl.multiple_of(e * quarter, 128), quarter)
                more = dot3(high_ref[:, here], low_ref[:, here], ph_ref[here], pl_ref[here], NN)
            if stage == 0:
                load_points(e, pts_ref, points_ref, arrived).wait()
                split_points(e, points_ref, ph_ref, pl_ref)
            if stage < 4:
                look_up(stage, e, *slots[stage % 2])
            if stage > 0:
                acc_ref[...] = more + jnp.where(e == 0, jnp.zeros_like(more), acc_ref[...])
            return carry

        if stage == 1:
            acc_ref[...] = jnp.zeros_like(acc_ref)
        lax.fori_loop(0, 4, part, 0)
        if stage > 0:
            for h in range(4):
                even = acc_ref[h * 64 : h * 64 + 32]
                odd = acc_ref[h * 64 + 32 : h * 64 + 64]
                keep_ref[(stage - 1) * 4 + h] = jnp.where(core == 0, even, odd)
                give_ref[(stage - 1) * 4 + h] = jnp.where(core == 0, odd, even)


def cross_part(place, points, mine, other, codes):
    count = points.shape[0]
    half = jax.ShapeDtypeStruct((16, 32, 256), F32)
    return pl.pallas_call(
        cross_kernel,
        out_shape=(half, half),
        in_specs=[SMEM, ANY, VMEM, VMEM] + [ANY] * len(codes),
        out_specs=(VMEM, VMEM),
        scratch_shapes=[
            pltpu.VMEM((M, count), jnp.int32),
            pltpu.VMEM((count, 256), F32),
            pltpu.VMEM((count, 256), BF16),
            pltpu.VMEM((count, 256), BF16),
            pltpu.VMEM((2, M // 2, SUB, K), F32),
            pltpu.VMEM((256, count), BF16),
            pltpu.VMEM((256, count), BF16),
            pltpu.VMEM((256, count), BF16),
            pltpu.VMEM((256, count), BF16),
            pltpu.VMEM((256, 256), F32),
            pltpu.SemaphoreType.DMA((8,)),
        ],
        compiler_params=grant(28),
        name="cross_part",
    )(place, points, mine, other, *codes)


def iterate_kernel(place_ref, mine_ref, other_ref, out_ref, now_ref, hl_ref, gh_ref, gl_ref, tail_ref, turned_ref):
    y, core, column = place_ref[0], place_ref[1], place_ref[2]
    total = jnp.zeros((1, 256), F32)
    for half, source in enumerate((mine_ref, other_ref)):
        for block in range(4):
            part = source[block * 16 : block * 16 + 16].reshape(512, 256)
            total += jnp.sum(part * part, axis=0, keepdims=True)
    scale = 1.7 / jnp.sqrt(jnp.sum(total, axis=1, keepdims=True) + 1e-06)
    for half, source in enumerate((mine_ref, other_ref)):
        for block in range(4):
            rows, columns = slice(half * 512, half * 512 + 512), slice(block * 256, block * 256 + 256)
            part = source[block * 16 : block * 16 + 16].reshape(512, 256) * scale
            now_ref[rows, columns] = part
            high, low = split(part)
            hl_ref[0, 0, rows, columns] = high
            hl_ref[0, 1, rows, columns] = low

    def step(k, carry):
        old, new = lax.rem(k, 2), 1 - lax.rem(k, 2)
        high_ref, low_ref = hl_ref.at[old, 0], hl_ref.at[old, 1]
        for j in range(4):
            strip, below = slice(j * 256, j * 256 + 256), slice(j * 256, D)
            gram = dot3(high_ref[below], low_ref[below], high_ref[strip], low_ref[strip], NT)
            high, low = split(gram)
            gh_ref[below, strip] = high
            gl_ref[below, strip] = low
            if j < 3:
                high, low = split(gram[256:].T)
                gh_ref[strip, j * 256 + 256 : D] = high
                gl_ref[strip, j * 256 + 256 : D] = low
        for j in range(4):
            strip = slice(j * 256, j * 256 + 256)
            moved = dot3(gh_ref[...], gl_ref[...], high_ref[:, strip], low_ref[:, strip], NN)
            value = 1.5 * now_ref[:, strip] - 0.5 * moved
            now_ref[:, strip] = value
            high, low = split(value)
            hl_ref[new, 0, :, strip] = high
            hl_ref[new, 1, :, strip] = low
        return carry

    lax.fori_loop(0, NS_ITERS - 1, step, 0)
    last = (NS_ITERS - 1) % 2
    high_ref, low_ref = hl_ref.at[last, 0], hl_ref.at[last, 1]
    columns = pl.ds(pl.multiple_of(column // 4 * 128, 128), 128)
    now = []
    for z in range(4):
        for c in range(2):
            half = lax.rem(c + core, 2)
            rows = pl.ds(pl.multiple_of(half * 512 + y * 128 + z * 32, 32), 32)
            here = slice(z * 64 + c * 32, z * 64 + c * 32 + 32)
            tail_ref[0, here] = high_ref[rows]
            tail_ref[1, here] = low_ref[rows]
            now.append(now_ref[rows, columns])
    gram = dot3(tail_ref[0], tail_ref[1], high_ref[...], low_ref[...], NT)
    high, low = split(gram)
    moved = dot3(high, low, high_ref[:, columns], low_ref[:, columns], NN)
    turned_ref[...] = ((1.5 * jnp.concatenate(now, axis=0) - 0.5 * moved) * D**0.5).T
    out_ref[...] = turned_ref[pl.ds(pl.multiple_of(lax.rem(column, 4) * 32, 32), 32), :]


def newton_schulz(place, mine, other):
    return pl.pallas_call(
        iterate_kernel,
        out_shape=jax.ShapeDtypeStruct((32, 256), F32),
        in_specs=[SMEM, VMEM, VMEM],
        out_specs=VMEM,
        scratch_shapes=[
            pltpu.VMEM((D, D), F32),
            pltpu.VMEM((2, 2, D, D), BF16),
            pltpu.VMEM((D, D), BF16),
            pltpu.VMEM((D, D), BF16),
            pltpu.VMEM((2, 256, D), BF16),
            pltpu.VMEM((128, 256), F32),
        ],
        compiler_params=grant(34),
        name="newton_schulz",
    )(place, mine, other)


def shards(points, codes, rotation):
    y, core = lax.axis_index("y"), lax.axis_index("core")
    own_row = lax.axis_index(ROWS)
    place = jnp.stack([y, core, own_row]).astype(jnp.int32)
    one, three = shift(codes, 1), shift(codes, 3)
    swapped = lax.ppermute(
        rotation, ("x", "y"), [(a * 4 + b, b * 4 + a) for a in range(4) for b in range(4)]
    )
    swapped, one, three = lax.optimization_barrier((swapped, one, three))
    pieces, two = spread_to(swapped, ("x", "z"), 16), shift(one, 1)
    pieces, two = lax.optimization_barrier((pieces, two))
    all_codes = [in_hbm(c) for c in (codes, one, two, three)]
    points = in_hbm(points)
    keep, give = code_sums(place, points, pieces, swap_core(pieces), all_codes)

    sums = keep + swap_core(give)
    sums = jnp.sum(lax.all_to_all(sums, CHIPS, 0, 0, tiled=True), axis=0)
    counts = sums[:2, K:].reshape(1, K)
    centers = spread_to(sums[:, :K] / counts, CHIPS, 64)
    others = swap_core(centers)

    keep, give = cross_part(place, points, centers, others, all_codes)
    block = keep + swap_core(give)
    block = jnp.sum(lax.all_to_all(block, ("x", "z"), 0, 0, tiled=True), axis=0)
    whole = spread_to(block, CHIPS, 64)
    ours = lax.dynamic_slice_in_dim(centers, y * 16, 16, axis=0)
    theirs = lax.dynamic_slice_in_dim(others, y * 16, 16, axis=0)
    first, second = jnp.where(core == 0, ours, theirs), jnp.where(core == 0, theirs, ours)
    centroids = jnp.stack([first, second], axis=1).transpose(0, 1, 3, 2).reshape(32, K * SUB)
    whole, centroids = lax.optimization_barrier((whole, centroids))
    rotated = newton_schulz(place, whole, swap_core(whole))
    return (rotated, centroids)


def solution(mesh):
    grid = Mesh(mesh.devices.reshape(4, 4, 2, 4), ("x", "z", "core", "y"))
    in_specs = (P(ROWS, "y"), P("y", ROWS), P(ROWS, "y"))
    out_specs = (P(ROWS, "y"), P("y", None))
    return jax.shard_map(shards, mesh=grid, in_specs=in_specs, out_specs=out_specs, check_vma=False)
```

```python
import functools

import jax
import jax.numpy as jnp
from jax import lax
from jax.experimental import pallas as pl
from jax.experimental.pallas import tpu as pltpu
from jax.sharding import Mesh, PartitionSpec as P

D = 1024
M = 128
K = 256
NS_ITERS = 6
SUB = 8
ROWS = ("x", "z", "core")
CHIPS = ("y", "x", "z")
BF16 = jnp.bfloat16
F32 = jnp.float32
NN = (((1,), (0,)), ((), ()))
NT = (((1,), (1,)), ((), ()))
VMEM = pl.BlockSpec(memory_space=pltpu.VMEM)
SMEM = pl.BlockSpec(memory_space=pltpu.SMEM)
ANY = pl.BlockSpec(memory_space=pl.ANY)


def grant(mebibytes):
    return pltpu.CompilerParams(vmem_limit_bytes=mebibytes * 1024 * 1024)


QUARTER = 98304 // 32 // 4
PAYLOAD = K * SUB // 2 + 128


def split(value):
    high = value.astype(BF16)
    return high, (value - high.astype(F32)).astype(BF16)


def mxu(left, right, dims):
    return lax.dot_general(left, right, dims, preferred_element_type=F32)


def dot3(left_high, left_low, right_high, right_low, dims):
    return (
        mxu(left_high, right_high, dims)
        + mxu(left_high, right_low, dims)
        + mxu(left_low, right_high, dims)
    )


def spread_to(value, axes, count):
    copies = jnp.broadcast_to(value[None], (count,) + value.shape)
    return lax.all_to_all(copies, axes, 0, 0, tiled=True)


def swap_core(value):
    return lax.ppermute(value, "core", [(0, 1), (1, 0)])


def in_hbm(value):
    return pltpu.with_memory_space_constraint(value, pltpu.HBM)


def shift(value, by):
    return lax.ppermute(value, "y", [(s, (s + by) % 4) for s in range(4)])


def at8(index):
    return pl.ds(pl.multiple_of(index * 8, 8), 8)


def fetch_codes(y, codes_ref, sources, arrived):
    copies = []
    for number, source in enumerate(sources):
        first = pl.multiple_of(lax.rem(y + 4 - number, 4) * 32, 32)
        target = codes_ref.at[pl.ds(first, 32), :]
        copies.append(pltpu.make_async_copy(source, target, arrived.at[number]))
    for copy in copies:
        copy.start()
    return copies


def load_points(i, pts_ref, points_ref, arrived):
    chunk = pl.ds(pl.multiple_of(i * QUARTER, QUARTER), QUARTER)
    return pltpu.make_async_copy(pts_ref.at[chunk], points_ref.at[chunk], arrived.at[4 + i])


def split_points(i, points_ref, ph_ref, pl_ref):
    chunk = pl.ds(pl.multiple_of(i * QUARTER, QUARTER), QUARTER)
    high, low = split(points_ref[chunk])
    ph_ref[chunk] = high
    pl_ref[chunk] = low


def sums_kernel(
    place_ref, pts_ref, first_ref, second_ref, c0, c1, c2, c3,
    keep_ref, give_ref, codes_ref, points_ref, ph_ref, pl_ref, panel_ref, rotated_ref, arrived,
):
    count = pts_ref.shape[0]
    y, core = place_ref[0], place_ref[1]
    for i in range(4):
        load_points(i, pts_ref, points_ref, arrived).start()
    copies = fetch_codes(y, codes_ref, (c0, c1, c2, c3), arrived)
    for a in range(4):
        for z in range(4):
            columns = slice(a * 256, a * 256 + 256)
            ours = pl.multiple_of(z * 64 + core * 32, 32)
            theirs = pl.multiple_of(z * 64 + (1 - core) * 32, 32)
            panel_ref[pl.ds(ours, 32), columns] = first_ref[a * 4 + z]
            panel_ref[pl.ds(theirs, 32), columns] = second_ref[a * 4 + z]

    for i in range(4):
        load_points(i, pts_ref, points_ref, arrived).wait()
        split_points(i, points_ref, ph_ref, pl_ref)

    def rotate(j, carry):
        panel = panel_ref[:, pl.ds(pl.multiple_of(j * 256, 256), 256)].T
        rh, rl = split(panel)
        part = dot3(rh, rl, ph_ref[...], pl_ref[...], NT)
        rotated_ref[pl.ds(j * 32, 32)] = part.reshape(32, SUB, count)
        return carry

    lax.fori_loop(0, D // 256, rotate, 0)
    for copy in copies:
        copy.wait()

    step = 512
    rows16 = lax.broadcasted_iota(jnp.int32, (16, step), 0).astype(F32)
    marks = [(rows16 + 16.0 * t).astype(BF16) for t in range(4)]
    tops = [jnp.full((16, step), t, BF16) for t in range(4)]
    one = jnp.ones((16, step), BF16)
    zero = jnp.zeros((16, step), BF16)
    lane = lax.broadcasted_iota(jnp.int32, (SUB, 128), 1)

    def pick(even, odd, mm):
        if mm % 2 == 0:
            odd = pltpu.roll(odd, 64, axis=1)
        else:
            even = pltpu.roll(even, 64, axis=1)
        return jnp.where(lane < 64, even, odd)

    def group(eight, quad, counted):
        total = jnp.zeros((288 if counted else 256, 256), F32)
        for n in range(0, count, step):
            lefts, rights = [], []
            rows = codes_ref[at8(eight), n : n + step]
            for mm in range(4):
                row = rows[quad * 4 + mm : quad * 4 + mm + 1]
                low = jnp.broadcast_to((row & 63).astype(F32), (16, step)).astype(BF16)
                top = jnp.broadcast_to((row >> 6).astype(F32), (16, step)).astype(BF16)
                value = rotated_ref[eight * 8 + quad * 4 + mm, :, n : n + step]
                high = value.astype(BF16).astype(F32)
                both = jnp.concatenate([high, value - high], axis=0).astype(BF16)
                for t in range(4):
                    lefts.append(jnp.where(top == tops[t], both, zero))
                    rights.append(jnp.where(low == marks[t], one, zero))
            if counted:
                tall = (rows >> 6).astype(F32)
                tall = jnp.concatenate([tall, tall], axis=0).astype(BF16)
                for t in range(2):
                    pattern = jnp.where(rows16 < 8, 2.0 * t, 2.0 * t + 1.0).astype(BF16)
                    lefts.append(jnp.where(tall == pattern, one, zero))
            total += mxu(jnp.concatenate(lefts, axis=0), jnp.concatenate(rights, axis=0), NT)
        found = []
        for mm in range(4):
            columns = slice((mm // 2) * 128, (mm // 2) * 128 + 128)
            slab = total[mm * 64 : mm * 64 + 64, columns]
            parts = [slab[t * 16 : t * 16 + 8] + slab[t * 16 + 8 : t * 16 + 16] for t in range(4)]
            halves = [pick(parts[2 * h], parts[2 * h + 1], mm) for h in range(2)]
            ticks = jnp.zeros((2, 128), F32)
            if counted:
                r = quad * 4 + mm
                tally = [total[256 + t * 8 : 264 + t * 8, columns] for t in range(4)]
                ticks = [pick(tally[2 * h], tally[2 * h + 1], mm)[r : r + 1] for h in range(2)]
                ticks = jnp.concatenate(ticks, axis=0)
            found.append(halves + [ticks])
        for h in range(2):
            q = eight * 4 + quad * 2 + h
            for number, (even, odd) in enumerate(zip(found[2 * h], found[2 * h + 1], strict=True)):
                for ref, value in (
                    (keep_ref, jnp.where(core == 0, even, odd)),
                    (give_ref, jnp.where(core == 0, odd, even)),
                ):
                    for i in range(value.shape[0] // 2):
                        lanes = slice((number * 4 + i) * 128, (number * 4 + i) * 128 + 128)
                        ref[q, :, lanes] = value[2 * i : 2 * i + 2]

    def eight_rows(i, carry, counted):
        eight = lax.rem(y * 4 + i, M // 8)
        group(eight, 0, counted)
        group(eight, 1, counted)
        return carry

    lax.fori_loop(0, 4, functools.partial(eight_rows, counted=True), 0)
    lax.fori_loop(4, M // 8, functools.partial(eight_rows, counted=False), 0)


def code_sums(place, points, first, second, codes):
    count = points.shape[0]
    half = jax.ShapeDtypeStruct((M // 2, 2, PAYLOAD), F32)
    return pl.pallas_call(
        sums_kernel,
        out_shape=(half, half),
        in_specs=[SMEM, ANY, VMEM, VMEM] + [ANY] * len(codes),
        out_specs=(VMEM, VMEM),
        scratch_shapes=[
            pltpu.VMEM((M, count), jnp.int32),
            pltpu.VMEM((count, 256), F32),
            pltpu.VMEM((count, 256), BF16),
            pltpu.VMEM((count, 256), BF16),
            pltpu.VMEM((256, D), F32),
            pltpu.VMEM((M, SUB, count), F32),
            pltpu.SemaphoreType.DMA((8,)),
        ],
        compiler_params=grant(34),
        name="code_sums",
    )(place, points, first, second, *codes)


def cross_kernel(
    place_ref, pts_ref, mine_ref, other_ref, c0, c1, c2, c3,
    keep_ref, give_ref,
    codes_ref, points_ref, ph_ref, pl_ref, tab_ref, ah0_ref, al0_ref, ah1_ref, al1_ref, acc_ref, arrived,
):
    count = pts_ref.shape[0]
    y, core = place_ref[0], place_ref[1]
    copies = fetch_codes(y, codes_ref, (c0, c1, c2, c3), arrived)
    for i in range(4):
        load_points(i, pts_ref, points_ref, arrived).start()
    tab_ref[core] = mine_ref[...]
    tab_ref[1 - core] = other_ref[...]
    for copy in copies:
        copy.wait()
    wide = 1024
    quarter = count // 4

    def look_up(block, eight, ah_ref, al_ref):
        for n in range(0, count, wide):
            rows = codes_ref[at8(block * 4 + eight), n : n + wide]
            for two in range(4):
                both = []
                for mm in range(2):
                    index = jnp.broadcast_to(rows[two * 2 + mm : two * 2 + mm + 1], (SUB, wide))
                    table = tab_ref[mm, block * 16 + eight * 4 + two]
                    found = []
                    for k in range(0, wide, 128):
                        here = index[:, k : k + 128]
                        inner = here & 127
                        first = jnp.take_along_axis(
                            table[:, :128], inner, axis=1, mode="promise_in_bounds"
                        )
                        second = jnp.take_along_axis(
                            table[:, 128:], inner, axis=1, mode="promise_in_bounds"
                        )
                        found.append(jnp.where(here < 128, first, second))
                    both.append(jnp.concatenate(found, axis=1))
                high, low = split(jnp.concatenate(both, axis=0))
                place = pl.ds(pl.multiple_of(eight * 64 + two * 16, 16), 16)
                ah_ref[place, n : n + wide] = high
                al_ref[place, n : n + wide] = low

    slots = ((ah0_ref, al0_ref), (ah1_ref, al1_ref))
    for stage in range(5):

        def part(e, carry, stage=stage):
            if stage > 0:
                high_ref, low_ref = slots[(stage - 1) % 2]
                here = pl.ds(pl.multiple_of(e * quarter, 128), quarter)
                more = dot3(high_ref[:, here], low_ref[:, here], ph_ref[here], pl_ref[here], NN)
            if stage == 0:
                load_points(e, pts_ref, points_ref, arrived).wait()
                split_points(e, points_ref, ph_ref, pl_ref)
            if stage < 4:
                look_up(stage, e, *slots[stage % 2])
            if stage > 0:
                acc_ref[...] = more + jnp.where(e == 0, jnp.zeros_like(more), acc_ref[...])
            return carry

        if stage == 1:
            acc_ref[...] = jnp.zeros_like(acc_ref)
        lax.fori_loop(0, 4, part, 0)
        if stage > 0:
            for h in range(4):
                even = acc_ref[h * 64 : h * 64 + 32]
                odd = acc_ref[h * 64 + 32 : h * 64 + 64]
                keep_ref[(stage - 1) * 4 + h] = jnp.where(core == 0, even, odd)
                give_ref[(stage - 1) * 4 + h] = jnp.where(core == 0, odd, even)


def cross_part(place, points, mine, other, codes):
    count = points.shape[0]
    half = jax.ShapeDtypeStruct((16, 32, 256), F32)
    return pl.pallas_call(
        cross_kernel,
        out_shape=(half, half),
        in_specs=[SMEM, ANY, VMEM, VMEM] + [ANY] * len(codes),
        out_specs=(VMEM, VMEM),
        scratch_shapes=[
            pltpu.VMEM((M, count), jnp.int32),
            pltpu.VMEM((count, 256), F32),
            pltpu.VMEM((count, 256), BF16),
            pltpu.VMEM((count, 256), BF16),
            pltpu.VMEM((2, M // 2, SUB, K), F32),
            pltpu.VMEM((256, count), BF16),
            pltpu.VMEM((256, count), BF16),
            pltpu.VMEM((256, count), BF16),
            pltpu.VMEM((256, count), BF16),
            pltpu.VMEM((256, 256), F32),
            pltpu.SemaphoreType.DMA((8,)),
        ],
        compiler_params=grant(28),
        name="cross_part",
    )(place, points, mine, other, *codes)


def iterate_kernel(place_ref, mine_ref, other_ref, out_ref, now_ref, hl_ref, gh_ref, gl_ref, tail_ref, turned_ref, mixed_ref):
    y, core, column = place_ref[0], place_ref[1], place_ref[2]
    total = jnp.zeros((1, 256), F32)
    for half, source in enumerate((mine_ref, other_ref)):
        for block in range(4):
            part = source[block * 16 : block * 16 + 16].reshape(512, 256)
            total += jnp.sum(part * part, axis=0, keepdims=True)
    scale = 1.7 / jnp.sqrt(jnp.sum(total, axis=1, keepdims=True) + 1e-06)
    for half, source in enumerate((mine_ref, other_ref)):
        for block in range(4):
            rows, columns = slice(half * 512, half * 512 + 512), slice(block * 256, block * 256 + 256)
            part = source[block * 16 : block * 16 + 16].reshape(512, 256) * scale
            now_ref[rows, columns] = part
            high, low = split(part)
            hl_ref[0, 0, rows, columns] = high
            hl_ref[0, 1, rows, columns] = low

    def step(k, carry):
        old, new = lax.rem(k, 2), 1 - lax.rem(k, 2)
        high_ref, low_ref = hl_ref.at[old, 0], hl_ref.at[old, 1]
        for j in range(4):
            strip = slice(j * 256, j * 256 + 256)
            mixed_ref[:, strip] = mxu(high_ref[...], low_ref[strip], NT)
        for j in range(4):
            strip, below = slice(j * 256, j * 256 + 256), slice(j * 256, D)
            gram = mxu(high_ref[below], high_ref[strip], NT)
            gram += mixed_ref[below, strip] + mixed_ref[strip, below].T
            high, low = split(gram)
            gh_ref[below, strip] = high
            gl_ref[below, strip] = low
            if j < 3:
                high, low = split(gram[256:].T)
                gh_ref[strip, j * 256 + 256 : D] = high
                gl_ref[strip, j * 256 + 256 : D] = low
        for j in range(4):
            strip = slice(j * 256, j * 256 + 256)
            moved = dot3(gh_ref[...], gl_ref[...], high_ref[:, strip], low_ref[:, strip], NN)
            value = 1.5 * now_ref[:, strip] - 0.5 * moved
            now_ref[:, strip] = value
            high, low = split(value)
            hl_ref[new, 0, :, strip] = high
            hl_ref[new, 1, :, strip] = low
        return carry

    lax.fori_loop(0, NS_ITERS - 1, step, 0)
    last = (NS_ITERS - 1) % 2
    high_ref, low_ref = hl_ref.at[last, 0], hl_ref.at[last, 1]
    columns = pl.ds(pl.multiple_of(column // 4 * 128, 128), 128)
    now = []
    for z in range(4):
        for c in range(2):
            half = lax.rem(c + core, 2)
            rows = pl.ds(pl.multiple_of(half * 512 + y * 128 + z * 32, 32), 32)
            here = slice(z * 64 + c * 32, z * 64 + c * 32 + 32)
            tail_ref[0, here] = high_ref[rows]
            tail_ref[1, here] = low_ref[rows]
            now.append(now_ref[rows, columns])
    gram = dot3(tail_ref[0], tail_ref[1], high_ref[...], low_ref[...], NT)
    high, low = split(gram)
    moved = dot3(high, low, high_ref[:, columns], low_ref[:, columns], NN)
    turned_ref[...] = ((1.5 * jnp.concatenate(now, axis=0) - 0.5 * moved) * D**0.5).T
    out_ref[...] = turned_ref[pl.ds(pl.multiple_of(lax.rem(column, 4) * 32, 32), 32), :]


def newton_schulz(place, mine, other):
    return pl.pallas_call(
        iterate_kernel,
        out_shape=jax.ShapeDtypeStruct((32, 256), F32),
        in_specs=[SMEM, VMEM, VMEM],
        out_specs=VMEM,
        scratch_shapes=[
            pltpu.VMEM((D, D), F32),
            pltpu.VMEM((2, 2, D, D), BF16),
            pltpu.VMEM((D, D), BF16),
            pltpu.VMEM((D, D), BF16),
            pltpu.VMEM((2, 256, D), BF16),
            pltpu.VMEM((128, 256), F32),
            pltpu.VMEM((D, D), F32),
        ],
        compiler_params=grant(34),
        name="newton_schulz",
    )(place, mine, other)


def shards(points, codes, rotation):
    y, core = lax.axis_index("y"), lax.axis_index("core")
    own_row = lax.axis_index(ROWS)
    place = jnp.stack([y, core, own_row]).astype(jnp.int32)
    one, three = shift(codes, 1), shift(codes, 3)
    swapped = lax.ppermute(
        rotation, ("x", "y"), [(a * 4 + b, b * 4 + a) for a in range(4) for b in range(4)]
    )
    swapped, one, three = lax.optimization_barrier((swapped, one, three))
    pieces, two = spread_to(swapped, ("x", "z"), 16), shift(one, 1)
    pieces, two = lax.optimization_barrier((pieces, two))
    all_codes = [in_hbm(c) for c in (codes, one, two, three)]
    points = in_hbm(points)
    keep, give = code_sums(place, points, pieces, swap_core(pieces), all_codes)

    sums = keep + swap_core(give)
    sums = jnp.sum(lax.all_to_all(sums, CHIPS, 0, 0, tiled=True), axis=0)
    counts = sums[:, PAYLOAD - 128 :].reshape(1, K)
    sums = sums[:, : PAYLOAD - 128].reshape(2, 2, 4, 128).transpose(2, 0, 1, 3).reshape(SUB, K)
    centers = spread_to(sums / counts, CHIPS, 64)
    others = swap_core(centers)

    keep, give = cross_part(place, points, centers, others, all_codes)
    block = keep + swap_core(give)
    block = jnp.sum(lax.all_to_all(block, ("x", "z"), 0, 0, tiled=True), axis=0)
    whole = spread_to(block, CHIPS, 64)
    ours = lax.dynamic_slice_in_dim(centers, y * 16, 16, axis=0)
    theirs = lax.dynamic_slice_in_dim(others, y * 16, 16, axis=0)
    first, second = jnp.where(core == 0, ours, theirs), jnp.where(core == 0, theirs, ours)
    centroids = jnp.stack([first, second], axis=1).transpose(0, 1, 3, 2).reshape(32, K * SUB)
    whole, centroids = lax.optimization_barrier((whole, centroids))
    rotated = newton_schulz(place, whole, swap_core(whole))
    return (rotated, centroids)


def solution(mesh):
    grid = Mesh(mesh.devices.reshape(4, 4, 2, 4), ("x", "z", "core", "y"))
    in_specs = (P(ROWS, "y"), P("y", ROWS), P(ROWS, "y"))
    out_specs = (P(ROWS, "y"), P("y", None))
    return jax.shard_map(shards, mesh=grid, in_specs=in_specs, out_specs=out_specs, check_vma=False)
```

```python
import functools

import jax
import jax.numpy as jnp
from jax import lax
from jax.experimental import pallas as pl
from jax.experimental.pallas import tpu as pltpu
from jax.sharding import Mesh, PartitionSpec as P

D = 1024
M = 128
K = 256
NS_ITERS = 6
SUB = 8
ROWS = ("x", "z", "core")
CHIPS = ("y", "x", "z")
BF16 = jnp.bfloat16
F32 = jnp.float32
NN = (((1,), (0,)), ((), ()))
NT = (((1,), (1,)), ((), ()))
VMEM = pl.BlockSpec(memory_space=pltpu.VMEM)
SMEM = pl.BlockSpec(memory_space=pltpu.SMEM)
ANY = pl.BlockSpec(memory_space=pl.ANY)


def grant(mebibytes):
    return pltpu.CompilerParams(vmem_limit_bytes=mebibytes * 1024 * 1024)


QUARTER = 98304 // 32 // 4
PAYLOAD = K * SUB // 2 + 128


def split(value):
    high = value.astype(BF16)
    return high, (value - high.astype(F32)).astype(BF16)


def mxu(left, right, dims):
    return lax.dot_general(left, right, dims, preferred_element_type=F32)


def dot3(left_high, left_low, right_high, right_low, dims):
    return (
        mxu(left_high, right_high, dims)
        + mxu(left_high, right_low, dims)
        + mxu(left_low, right_high, dims)
    )


def spread_to(value, axes, count):
    copies = jnp.broadcast_to(value[None], (count,) + value.shape)
    return lax.all_to_all(copies, axes, 0, 0, tiled=True)


def swap_core(value):
    return lax.ppermute(value, "core", [(0, 1), (1, 0)])


def in_hbm(value):
    return pltpu.with_memory_space_constraint(value, pltpu.HBM)


def shift(value, by):
    return lax.ppermute(value, "y", [(s, (s + by) % 4) for s in range(4)])


def at8(index):
    return pl.ds(pl.multiple_of(index * 8, 8), 8)


def fetch_codes(y, codes_ref, sources, arrived):
    copies = []
    for number, source in enumerate(sources):
        first = pl.multiple_of(lax.rem(y + 4 - number, 4) * 32, 32)
        target = codes_ref.at[pl.ds(first, 32), :]
        copies.append(pltpu.make_async_copy(source, target, arrived.at[number]))
    for copy in copies:
        copy.start()
    return copies


def load_points(i, pts_ref, points_ref, arrived):
    chunk = pl.ds(pl.multiple_of(i * QUARTER, QUARTER), QUARTER)
    return pltpu.make_async_copy(pts_ref.at[chunk], points_ref.at[chunk], arrived.at[4 + i])


def split_points(i, points_ref, ph_ref, pl_ref):
    chunk = pl.ds(pl.multiple_of(i * QUARTER, QUARTER), QUARTER)
    high, low = split(points_ref[chunk])
    ph_ref[chunk] = high
    pl_ref[chunk] = low


def sums_kernel(
    place_ref, pts_ref, first_ref, second_ref, c0, c1, c2, c3,
    keep_ref, give_ref, codes_ref, points_ref, ph_ref, pl_ref, panel_ref, rotated_ref, arrived,
):
    count = pts_ref.shape[0]
    y, core = place_ref[0], place_ref[1]
    for i in range(4):
        load_points(i, pts_ref, points_ref, arrived).start()
    copies = fetch_codes(y, codes_ref, (c0, c1, c2, c3), arrived)
    for a in range(4):
        for z in range(4):
            columns = slice(a * 256, a * 256 + 256)
            ours = pl.multiple_of(z * 64 + core * 32, 32)
            theirs = pl.multiple_of(z * 64 + (1 - core) * 32, 32)
            panel_ref[pl.ds(ours, 32), columns] = first_ref[a * 4 + z]
            panel_ref[pl.ds(theirs, 32), columns] = second_ref[a * 4 + z]

    for i in range(4):
        load_points(i, pts_ref, points_ref, arrived).wait()
        split_points(i, points_ref, ph_ref, pl_ref)

    def rotate(j, carry):
        panel = panel_ref[:, pl.ds(pl.multiple_of(j * 256, 256), 256)].T
        rh, rl = split(panel)
        part = dot3(rh, rl, ph_ref[...], pl_ref[...], NT)
        rotated_ref[pl.ds(j * 32, 32)] = part.reshape(32, SUB, count)
        return carry

    lax.fori_loop(0, D // 256, rotate, 0, unroll=2)
    for copy in copies:
        copy.wait()

    step = 512
    rows16 = lax.broadcasted_iota(jnp.int32, (16, step), 0).astype(F32)
    marks = [(rows16 + 16.0 * t).astype(BF16) for t in range(4)]
    tops = [jnp.full((16, step), t, BF16) for t in range(4)]
    one = jnp.ones((16, step), BF16)
    zero = jnp.zeros((16, step), BF16)
    lane = lax.broadcasted_iota(jnp.int32, (SUB, 128), 1)

    def pick(even, odd, mm):
        if mm % 2 == 0:
            odd = pltpu.roll(odd, 64, axis=1)
        else:
            even = pltpu.roll(even, 64, axis=1)
        return jnp.where(lane < 64, even, odd)

    def group(eight, quad, counted):
        total = jnp.zeros((288 if counted else 256, 256), F32)
        for n in range(0, count, step):
            lefts, rights = [], []
            rows = codes_ref[at8(eight), n : n + step]
            for mm in range(4):
                row = rows[quad * 4 + mm : quad * 4 + mm + 1]
                low = jnp.broadcast_to((row & 63).astype(F32), (16, step)).astype(BF16)
                top = jnp.broadcast_to((row >> 6).astype(F32), (16, step)).astype(BF16)
                value = rotated_ref[eight * 8 + quad * 4 + mm, :, n : n + step]
                high = value.astype(BF16).astype(F32)
                both = jnp.concatenate([high, value - high], axis=0).astype(BF16)
                for t in range(4):
                    lefts.append(jnp.where(top == tops[t], both, zero))
                    rights.append(jnp.where(low == marks[t], one, zero))
            if counted:
                tall = (rows >> 6).astype(F32)
                tall = jnp.concatenate([tall, tall], axis=0).astype(BF16)
                for t in range(2):
                    pattern = jnp.where(rows16 < 8, 2.0 * t, 2.0 * t + 1.0).astype(BF16)
                    lefts.append(jnp.where(tall == pattern, one, zero))
            total += mxu(jnp.concatenate(lefts, axis=0), jnp.concatenate(rights, axis=0), NT)
        found = []
        for mm in range(4):
            columns = slice((mm // 2) * 128, (mm // 2) * 128 + 128)
            slab = total[mm * 64 : mm * 64 + 64, columns]
            parts = [slab[t * 16 : t * 16 + 8] + slab[t * 16 + 8 : t * 16 + 16] for t in range(4)]
            halves = [pick(parts[2 * h], parts[2 * h + 1], mm) for h in range(2)]
            ticks = jnp.zeros((2, 128), F32)
            if counted:
                r = quad * 4 + mm
                tally = [total[256 + t * 8 : 264 + t * 8, columns] for t in range(4)]
                ticks = [pick(tally[2 * h], tally[2 * h + 1], mm)[r : r + 1] for h in range(2)]
                ticks = jnp.concatenate(ticks, axis=0)
            found.append(halves + [ticks])
        for h in range(2):
            q = eight * 4 + quad * 2 + h
            for number, (even, odd) in enumerate(zip(found[2 * h], found[2 * h + 1], strict=True)):
                for ref, value in (
                    (keep_ref, jnp.where(core == 0, even, odd)),
                    (give_ref, jnp.where(core == 0, odd, even)),
                ):
                    for i in range(value.shape[0] // 2):
                        lanes = slice((number * 4 + i) * 128, (number * 4 + i) * 128 + 128)
                        ref[q, :, lanes] = value[2 * i : 2 * i + 2]

    def eight_rows(i, carry, counted):
        eight = lax.rem(y * 4 + i, M // 8)
        group(eight, 0, counted)
        group(eight, 1, counted)
        return carry

    lax.fori_loop(0, 4, functools.partial(eight_rows, counted=True), 0, unroll=2)
    lax.fori_loop(4, M // 8, functools.partial(eight_rows, counted=False), 0, unroll=2)


def code_sums(place, points, first, second, codes):
    count = points.shape[0]
    half = jax.ShapeDtypeStruct((M // 2, 2, PAYLOAD), F32)
    return pl.pallas_call(
        sums_kernel,
        out_shape=(half, half),
        in_specs=[SMEM, ANY, VMEM, VMEM] + [ANY] * len(codes),
        out_specs=(VMEM, VMEM),
        scratch_shapes=[
            pltpu.VMEM((M, count), jnp.int32),
            pltpu.VMEM((count, 256), F32),
            pltpu.VMEM((count, 256), BF16),
            pltpu.VMEM((count, 256), BF16),
            pltpu.VMEM((256, D), F32),
            pltpu.VMEM((M, SUB, count), F32),
            pltpu.SemaphoreType.DMA((8,)),
        ],
        compiler_params=grant(34),
        name="code_sums",
    )(place, points, first, second, *codes)


def cross_kernel(
    place_ref, pts_ref, mine_ref, other_ref, c0, c1, c2, c3,
    keep_ref, give_ref,
    codes_ref, points_ref, ph_ref, pl_ref, tab_ref, ah0_ref, al0_ref, ah1_ref, al1_ref, acc_ref, arrived,
):
    count = pts_ref.shape[0]
    y, core = place_ref[0], place_ref[1]
    copies = fetch_codes(y, codes_ref, (c0, c1, c2, c3), arrived)
    for i in range(4):
        load_points(i, pts_ref, points_ref, arrived).start()
    tab_ref[core] = mine_ref[...]
    tab_ref[1 - core] = other_ref[...]
    for copy in copies:
        copy.wait()
    wide = 1024
    quarter = count // 4

    def look_up(block, eight, ah_ref, al_ref):
        for n in range(0, count, wide):
            rows = codes_ref[at8(block * 4 + eight), n : n + wide]
            for two in range(4):
                both = []
                for mm in range(2):
                    index = jnp.broadcast_to(rows[two * 2 + mm : two * 2 + mm + 1], (SUB, wide))
                    table = tab_ref[mm, block * 16 + eight * 4 + two]
                    found = []
                    for k in range(0, wide, 128):
                        here = index[:, k : k + 128]
                        inner = here & 127
                        first = jnp.take_along_axis(
                            table[:, :128], inner, axis=1, mode="promise_in_bounds"
                        )
                        second = jnp.take_along_axis(
                            table[:, 128:], inner, axis=1, mode="promise_in_bounds"
                        )
                        found.append(jnp.where(here < 128, first, second))
                    both.append(jnp.concatenate(found, axis=1))
                high, low = split(jnp.concatenate(both, axis=0))
                place = pl.ds(pl.multiple_of(eight * 64 + two * 16, 16), 16)
                ah_ref[place, n : n + wide] = high
                al_ref[place, n : n + wide] = low

    slots = ((ah0_ref, al0_ref), (ah1_ref, al1_ref))
    for stage in range(5):

        def part(e, carry, stage=stage):
            if stage > 0:
                high_ref, low_ref = slots[(stage - 1) % 2]
                here = pl.ds(pl.multiple_of(e * quarter, 128), quarter)
                more = dot3(high_ref[:, here], low_ref[:, here], ph_ref[here], pl_ref[here], NN)
            if stage == 0:
                load_points(e, pts_ref, points_ref, arrived).wait()
                split_points(e, points_ref, ph_ref, pl_ref)
            if stage < 4:
                look_up(stage, e, *slots[stage % 2])
            if stage > 0:
                acc_ref[...] = more + jnp.where(e == 0, jnp.zeros_like(more), acc_ref[...])
            return carry

        if stage == 1:
            acc_ref[...] = jnp.zeros_like(acc_ref)
        lax.fori_loop(0, 4, part, 0, unroll=4)
        if stage > 0:
            for h in range(4):
                even = acc_ref[h * 64 : h * 64 + 32]
                odd = acc_ref[h * 64 + 32 : h * 64 + 64]
                keep_ref[(stage - 1) * 4 + h] = jnp.where(core == 0, even, odd)
                give_ref[(stage - 1) * 4 + h] = jnp.where(core == 0, odd, even)


def cross_part(place, points, mine, other, codes):
    count = points.shape[0]
    half = jax.ShapeDtypeStruct((16, 32, 256), F32)
    return pl.pallas_call(
        cross_kernel,
        out_shape=(half, half),
        in_specs=[SMEM, ANY, VMEM, VMEM] + [ANY] * len(codes),
        out_specs=(VMEM, VMEM),
        scratch_shapes=[
            pltpu.VMEM((M, count), jnp.int32),
            pltpu.VMEM((count, 256), F32),
            pltpu.VMEM((count, 256), BF16),
            pltpu.VMEM((count, 256), BF16),
            pltpu.VMEM((2, M // 2, SUB, K), F32),
            pltpu.VMEM((256, count), BF16),
            pltpu.VMEM((256, count), BF16),
            pltpu.VMEM((256, count), BF16),
            pltpu.VMEM((256, count), BF16),
            pltpu.VMEM((256, 256), F32),
            pltpu.SemaphoreType.DMA((8,)),
        ],
        compiler_params=grant(28),
        name="cross_part",
    )(place, points, mine, other, *codes)


def iterate_kernel(place_ref, mine_ref, other_ref, out_ref, now_ref, hl_ref, gh_ref, gl_ref, tail_ref, turned_ref, mixed_ref):
    y, core, column = place_ref[0], place_ref[1], place_ref[2]
    total = jnp.zeros((1, 256), F32)
    for half, source in enumerate((mine_ref, other_ref)):
        for block in range(4):
            part = source[block * 16 : block * 16 + 16].reshape(512, 256)
            total += jnp.sum(part * part, axis=0, keepdims=True)
    scale = 1.7 / jnp.sqrt(jnp.sum(total, axis=1, keepdims=True) + 1e-06)
    for half, source in enumerate((mine_ref, other_ref)):
        for block in range(4):
            rows, columns = slice(half * 512, half * 512 + 512), slice(block * 256, block * 256 + 256)
            part = source[block * 16 : block * 16 + 16].reshape(512, 256) * scale
            now_ref[rows, columns] = part
            high, low = split(part)
            hl_ref[0, 0, rows, columns] = high
            hl_ref[0, 1, rows, columns] = low

    def step(k, carry):
        old, new = lax.rem(k, 2), 1 - lax.rem(k, 2)
        high_ref, low_ref = hl_ref.at[old, 0], hl_ref.at[old, 1]
        for j in range(4):
            strip = slice(j * 256, j * 256 + 256)
            mixed_ref[:, strip] = mxu(high_ref[...], low_ref[strip], NT)
        for j in range(4):
            strip, below = slice(j * 256, j * 256 + 256), slice(j * 256, D)
            gram = mxu(high_ref[below], high_ref[strip], NT)
            gram += mixed_ref[below, strip] + mixed_ref[strip, below].T
            high, low = split(gram)
            gh_ref[below, strip] = high
            gl_ref[below, strip] = low
            if j < 3:
                high, low = split(gram[256:].T)
                gh_ref[strip, j * 256 + 256 : D] = high
                gl_ref[strip, j * 256 + 256 : D] = low
        for j in range(4):
            strip = slice(j * 256, j * 256 + 256)
            moved = dot3(gh_ref[...], gl_ref[...], high_ref[:, strip], low_ref[:, strip], NN)
            value = 1.5 * now_ref[:, strip] - 0.5 * moved
            now_ref[:, strip] = value
            high, low = split(value)
            hl_ref[new, 0, :, strip] = high
            hl_ref[new, 1, :, strip] = low
        return carry

    lax.fori_loop(0, NS_ITERS - 1, step, 0)
    last = (NS_ITERS - 1) % 2
    high_ref, low_ref = hl_ref.at[last, 0], hl_ref.at[last, 1]
    columns = pl.ds(pl.multiple_of(column // 4 * 128, 128), 128)
    now = []
    for z in range(4):
        for c in range(2):
            half = lax.rem(c + core, 2)
            rows = pl.ds(pl.multiple_of(half * 512 + y * 128 + z * 32, 32), 32)
            here = slice(z * 64 + c * 32, z * 64 + c * 32 + 32)
            tail_ref[0, here] = high_ref[rows]
            tail_ref[1, here] = low_ref[rows]
            now.append(now_ref[rows, columns])
    gram = dot3(tail_ref[0], tail_ref[1], high_ref[...], low_ref[...], NT)
    high, low = split(gram)
    moved = dot3(high, low, high_ref[:, columns], low_ref[:, columns], NN)
    turned_ref[...] = ((1.5 * jnp.concatenate(now, axis=0) - 0.5 * moved) * D**0.5).T
    out_ref[...] = turned_ref[pl.ds(pl.multiple_of(lax.rem(column, 4) * 32, 32), 32), :]


def newton_schulz(place, mine, other):
    return pl.pallas_call(
        iterate_kernel,
        out_shape=jax.ShapeDtypeStruct((32, 256), F32),
        in_specs=[SMEM, VMEM, VMEM],
        out_specs=VMEM,
        scratch_shapes=[
            pltpu.VMEM((D, D), F32),
            pltpu.VMEM((2, 2, D, D), BF16),
            pltpu.VMEM((D, D), BF16),
            pltpu.VMEM((D, D), BF16),
            pltpu.VMEM((2, 256, D), BF16),
            pltpu.VMEM((128, 256), F32),
            pltpu.VMEM((D, D), F32),
        ],
        compiler_params=grant(34),
        name="newton_schulz",
    )(place, mine, other)


def shards(points, codes, rotation):
    y, core = lax.axis_index("y"), lax.axis_index("core")
    own_row = lax.axis_index(ROWS)
    place = jnp.stack([y, core, own_row]).astype(jnp.int32)
    one, three = shift(codes, 1), shift(codes, 3)
    swapped = lax.ppermute(
        rotation, ("x", "y"), [(a * 4 + b, b * 4 + a) for a in range(4) for b in range(4)]
    )
    swapped, one, three = lax.optimization_barrier((swapped, one, three))
    pieces, two = spread_to(swapped, ("x", "z"), 16), shift(one, 1)
    pieces, two = lax.optimization_barrier((pieces, two))
    all_codes = [in_hbm(c) for c in (codes, one, two, three)]
    points = in_hbm(points)
    keep, give = code_sums(place, points, pieces, swap_core(pieces), all_codes)

    sums = keep + swap_core(give)
    sums = jnp.sum(lax.all_to_all(sums, CHIPS, 0, 0, tiled=True), axis=0)
    counts = sums[:, PAYLOAD - 128 :].reshape(1, K)
    sums = sums[:, : PAYLOAD - 128].reshape(2, 2, 4, 128).transpose(2, 0, 1, 3).reshape(SUB, K)
    centers = spread_to(sums / counts, CHIPS, 64)
    others = swap_core(centers)

    keep, give = cross_part(place, points, centers, others, all_codes)
    block = keep + swap_core(give)
    block = jnp.sum(lax.all_to_all(block, ("x", "z"), 0, 0, tiled=True), axis=0)
    whole = spread_to(block, CHIPS, 64)
    ours = lax.dynamic_slice_in_dim(centers, y * 16, 16, axis=0)
    theirs = lax.dynamic_slice_in_dim(others, y * 16, 16, axis=0)
    first, second = jnp.where(core == 0, ours, theirs), jnp.where(core == 0, theirs, ours)
    centroids = jnp.stack([first, second], axis=1).transpose(0, 1, 3, 2).reshape(32, K * SUB)
    whole, centroids = lax.optimization_barrier((whole, centroids))
    rotated = newton_schulz(place, whole, swap_core(whole))
    return (rotated, centroids)


def solution(mesh):
    grid = Mesh(mesh.devices.reshape(4, 4, 2, 4), ("x", "z", "core", "y"))
    in_specs = (P(ROWS, "y"), P("y", ROWS), P(ROWS, "y"))
    out_specs = (P(ROWS, "y"), P("y", None))
    return jax.shard_map(shards, mesh=grid, in_specs=in_specs, out_specs=out_specs, check_vma=False)
```

```python
import functools

import jax
import jax.numpy as jnp
from jax import lax
from jax.experimental import pallas as pl
from jax.experimental.pallas import tpu as pltpu
from jax.sharding import Mesh, PartitionSpec as P

D = 1024
M = 128
K = 256
NS_ITERS = 6
SUB = 8
ROWS = ("x", "z", "core")
CHIPS = ("y", "x", "z")
BF16 = jnp.bfloat16
F32 = jnp.float32
NN = (((1,), (0,)), ((), ()))
NT = (((1,), (1,)), ((), ()))
VMEM = pl.BlockSpec(memory_space=pltpu.VMEM)
SMEM = pl.BlockSpec(memory_space=pltpu.SMEM)
ANY = pl.BlockSpec(memory_space=pl.ANY)


def grant(mebibytes):
    return pltpu.CompilerParams(vmem_limit_bytes=mebibytes * 1024 * 1024)


QUARTER = 98304 // 32 // 4
PAYLOAD = K * SUB // 2 + 128


def split(value):
    high = value.astype(BF16)
    return high, (value - high.astype(F32)).astype(BF16)


def mxu(left, right, dims):
    return lax.dot_general(left, right, dims, preferred_element_type=F32)


def dot3(left_high, left_low, right_high, right_low, dims):
    return (
        mxu(left_high, right_high, dims)
        + mxu(left_high, right_low, dims)
        + mxu(left_low, right_high, dims)
    )


def spread_to(value, axes, count):
    copies = jnp.broadcast_to(value[None], (count,) + value.shape)
    return lax.all_to_all(copies, axes, 0, 0, tiled=True)


def swap_core(value):
    return lax.ppermute(value, "core", [(0, 1), (1, 0)])


def in_hbm(value):
    return pltpu.with_memory_space_constraint(value, pltpu.HBM)


def shift(value, by):
    return lax.ppermute(value, "y", [(s, (s + by) % 4) for s in range(4)])


def at8(index):
    return pl.ds(pl.multiple_of(index * 8, 8), 8)


def fetch_codes(y, codes_ref, sources, arrived):
    copies = []
    for number, source in enumerate(sources):
        first = pl.multiple_of(lax.rem(y + 4 - number, 4) * 32, 32)
        target = codes_ref.at[pl.ds(first, 32), :]
        copies.append(pltpu.make_async_copy(source, target, arrived.at[number]))
    for copy in copies:
        copy.start()
    return copies


def load_points(i, pts_ref, points_ref, arrived):
    chunk = pl.ds(pl.multiple_of(i * QUARTER, QUARTER), QUARTER)
    return pltpu.make_async_copy(pts_ref.at[chunk], points_ref.at[chunk], arrived.at[4 + i])


def split_points(i, points_ref, ph_ref, pl_ref):
    chunk = pl.ds(pl.multiple_of(i * QUARTER, QUARTER), QUARTER)
    high, low = split(points_ref[chunk])
    ph_ref[chunk] = high
    pl_ref[chunk] = low


def sums_kernel(
    place_ref, pts_ref, first_ref, second_ref, c0, c1, c2, c3,
    keep_ref, give_ref, codes_ref, points_ref, ph_ref, pl_ref, panel_ref, rotated_ref, arrived,
):
    count = pts_ref.shape[0]
    y, core = place_ref[0], place_ref[1]
    for i in range(4):
        load_points(i, pts_ref, points_ref, arrived).start()
    copies = fetch_codes(y, codes_ref, (c0, c1, c2, c3), arrived)
    for a in range(4):
        for z in range(4):
            columns = slice(a * 256, a * 256 + 256)
            ours = pl.multiple_of(z * 64 + core * 32, 32)
            theirs = pl.multiple_of(z * 64 + (1 - core) * 32, 32)
            panel_ref[pl.ds(ours, 32), columns] = first_ref[a * 4 + z]
            panel_ref[pl.ds(theirs, 32), columns] = second_ref[a * 4 + z]

    for i in range(4):
        load_points(i, pts_ref, points_ref, arrived).wait()
        split_points(i, points_ref, ph_ref, pl_ref)

    def rotate(j, carry):
        panel = panel_ref[:, pl.ds(pl.multiple_of(j * 256, 256), 256)].T
        rh, rl = split(panel)
        part = dot3(rh, rl, ph_ref[...], pl_ref[...], NT)
        rotated_ref[pl.ds(j * 32, 32)] = part.reshape(32, SUB, count)
        return carry

    lax.fori_loop(0, D // 256, rotate, 0)
    for copy in copies:
        copy.wait()

    step = 512
    rows16 = lax.broadcasted_iota(jnp.int32, (16, step), 0).astype(F32)
    marks = [(rows16 + 16.0 * t).astype(BF16) for t in range(4)]
    tops = [jnp.full((16, step), t, BF16) for t in range(4)]
    one = jnp.ones((16, step), BF16)
    zero = jnp.zeros((16, step), BF16)
    lane = lax.broadcasted_iota(jnp.int32, (SUB, 128), 1)

    def pick(even, odd, mm):
        if mm % 2 == 0:
            odd = pltpu.roll(odd, 64, axis=1)
        else:
            even = pltpu.roll(even, 64, axis=1)
        return jnp.where(lane < 64, even, odd)

    def group(eight, quad, counted):
        total = jnp.zeros((288 if counted else 256, 256), F32)
        for n in range(0, count, step):
            lefts, rights = [], []
            rows = codes_ref[at8(eight), n : n + step]
            for mm in range(4):
                row = rows[quad * 4 + mm : quad * 4 + mm + 1]
                low = jnp.broadcast_to((row & 63).astype(F32), (16, step)).astype(BF16)
                top = jnp.broadcast_to((row >> 6).astype(F32), (16, step)).astype(BF16)
                value = rotated_ref[eight * 8 + quad * 4 + mm, :, n : n + step]
                high = value.astype(BF16).astype(F32)
                both = jnp.concatenate([high, value - high], axis=0).astype(BF16)
                for t in range(4):
                    lefts.append(jnp.where(top == tops[t], both, zero))
                    rights.append(jnp.where(low == marks[t], one, zero))
            if counted:
                tall = (rows >> 6).astype(F32)
                tall = jnp.concatenate([tall, tall], axis=0).astype(BF16)
                for t in range(2):
                    pattern = jnp.where(rows16 < 8, 2.0 * t, 2.0 * t + 1.0).astype(BF16)
                    lefts.append(jnp.where(tall == pattern, one, zero))
            total += mxu(jnp.concatenate(lefts, axis=0), jnp.concatenate(rights, axis=0), NT)
        found = []
        for mm in range(4):
            columns = slice((mm // 2) * 128, (mm // 2) * 128 + 128)
            slab = total[mm * 64 : mm * 64 + 64, columns]
            parts = [slab[t * 16 : t * 16 + 8] + slab[t * 16 + 8 : t * 16 + 16] for t in range(4)]
            halves = [pick(parts[2 * h], parts[2 * h + 1], mm) for h in range(2)]
            ticks = jnp.zeros((2, 128), F32)
            if counted:
                r = quad * 4 + mm
                tally = [total[256 + t * 8 : 264 + t * 8, columns] for t in range(4)]
                ticks = [pick(tally[2 * h], tally[2 * h + 1], mm)[r : r + 1] for h in range(2)]
                ticks = jnp.concatenate(ticks, axis=0)
            found.append(halves + [ticks])
        for h in range(2):
            q = eight * 4 + quad * 2 + h
            for number, (even, odd) in enumerate(zip(found[2 * h], found[2 * h + 1], strict=True)):
                for ref, value in (
                    (keep_ref, jnp.where(core == 0, even, odd)),
                    (give_ref, jnp.where(core == 0, odd, even)),
                ):
                    for i in range(value.shape[0] // 2):
                        lanes = slice((number * 4 + i) * 128, (number * 4 + i) * 128 + 128)
                        ref[q, :, lanes] = value[2 * i : 2 * i + 2]

    def eight_rows(i, carry, counted):
        eight = lax.rem(y * 4 + i, M // 8)
        group(eight, 0, counted)
        group(eight, 1, counted)
        return carry

    lax.fori_loop(0, 4, functools.partial(eight_rows, counted=True), 0)
    lax.fori_loop(4, M // 8, functools.partial(eight_rows, counted=False), 0, unroll=2)


def code_sums(place, points, first, second, codes):
    count = points.shape[0]
    half = jax.ShapeDtypeStruct((M // 2, 2, PAYLOAD), F32)
    return pl.pallas_call(
        sums_kernel,
        out_shape=(half, half),
        in_specs=[SMEM, ANY, VMEM, VMEM] + [ANY] * len(codes),
        out_specs=(VMEM, VMEM),
        scratch_shapes=[
            pltpu.VMEM((M, count), jnp.int32),
            pltpu.VMEM((count, 256), F32),
            pltpu.VMEM((count, 256), BF16),
            pltpu.VMEM((count, 256), BF16),
            pltpu.VMEM((256, D), F32),
            pltpu.VMEM((M, SUB, count), F32),
            pltpu.SemaphoreType.DMA((8,)),
        ],
        compiler_params=grant(34),
        name="code_sums",
    )(place, points, first, second, *codes)


def cross_kernel(
    place_ref, pts_ref, mine_ref, other_ref, c0, c1, c2, c3,
    keep_ref, give_ref,
    codes_ref, points_ref, ph_ref, pl_ref, tab_ref, ah0_ref, al0_ref, ah1_ref, al1_ref, acc_ref, arrived,
):
    count = pts_ref.shape[0]
    y, core = place_ref[0], place_ref[1]
    copies = fetch_codes(y, codes_ref, (c0, c1, c2, c3), arrived)
    for i in range(4):
        load_points(i, pts_ref, points_ref, arrived).start()
    tab_ref[core] = mine_ref[...]
    tab_ref[1 - core] = other_ref[...]
    for copy in copies:
        copy.wait()
    wide = 1024
    quarter = count // 4

    def look_up(block, eight, ah_ref, al_ref):
        for n in range(0, count, wide):
            rows = codes_ref[at8(block * 4 + eight), n : n + wide]
            for two in range(4):
                both = []
                for mm in range(2):
                    index = jnp.broadcast_to(rows[two * 2 + mm : two * 2 + mm + 1], (SUB, wide))
                    table = tab_ref[mm, block * 16 + eight * 4 + two]
                    found = []
                    for k in range(0, wide, 128):
                        here = index[:, k : k + 128]
                        inner = here & 127
                        first = jnp.take_along_axis(
                            table[:, :128], inner, axis=1, mode="promise_in_bounds"
                        )
                        second = jnp.take_along_axis(
                            table[:, 128:], inner, axis=1, mode="promise_in_bounds"
                        )
                        found.append(jnp.where(here < 128, first, second))
                    both.append(jnp.concatenate(found, axis=1))
                high, low = split(jnp.concatenate(both, axis=0))
                place = pl.ds(pl.multiple_of(eight * 64 + two * 16, 16), 16)
                ah_ref[place, n : n + wide] = high
                al_ref[place, n : n + wide] = low

    slots = ((ah0_ref, al0_ref), (ah1_ref, al1_ref))
    for stage in range(5):

        def part(e, carry, stage=stage):
            if stage > 0:
                high_ref, low_ref = slots[(stage - 1) % 2]
                here = pl.ds(pl.multiple_of(e * quarter, 128), quarter)
                more = dot3(high_ref[:, here], low_ref[:, here], ph_ref[here], pl_ref[here], NN)
            if stage == 0:
                load_points(e, pts_ref, points_ref, arrived).wait()
                split_points(e, points_ref, ph_ref, pl_ref)
            if stage < 4:
                look_up(stage, e, *slots[stage % 2])
            if stage > 0:
                acc_ref[...] = more + jnp.where(e == 0, jnp.zeros_like(more), acc_ref[...])
            return carry

        if stage == 1:
            acc_ref[...] = jnp.zeros_like(acc_ref)
        lax.fori_loop(0, 4, part, 0, unroll=2 if 0 < stage < 4 else 1)
        if stage > 0:
            for h in range(4):
                even = acc_ref[h * 64 : h * 64 + 32]
                odd = acc_ref[h * 64 + 32 : h * 64 + 64]
                keep_ref[(stage - 1) * 4 + h] = jnp.where(core == 0, even, odd)
                give_ref[(stage - 1) * 4 + h] = jnp.where(core == 0, odd, even)


def cross_part(place, points, mine, other, codes):
    count = points.shape[0]
    half = jax.ShapeDtypeStruct((16, 32, 256), F32)
    return pl.pallas_call(
        cross_kernel,
        out_shape=(half, half),
        in_specs=[SMEM, ANY, VMEM, VMEM] + [ANY] * len(codes),
        out_specs=(VMEM, VMEM),
        scratch_shapes=[
            pltpu.VMEM((M, count), jnp.int32),
            pltpu.VMEM((count, 256), F32),
            pltpu.VMEM((count, 256), BF16),
            pltpu.VMEM((count, 256), BF16),
            pltpu.VMEM((2, M // 2, SUB, K), F32),
            pltpu.VMEM((256, count), BF16),
            pltpu.VMEM((256, count), BF16),
            pltpu.VMEM((256, count), BF16),
            pltpu.VMEM((256, count), BF16),
            pltpu.VMEM((256, 256), F32),
            pltpu.SemaphoreType.DMA((8,)),
        ],
        compiler_params=grant(28),
        name="cross_part",
    )(place, points, mine, other, *codes)


def iterate_kernel(place_ref, mine_ref, other_ref, out_ref, now_ref, hl_ref, gh_ref, gl_ref, tail_ref, turned_ref, mixed_ref):
    y, core, column = place_ref[0], place_ref[1], place_ref[2]
    total = jnp.zeros((1, 256), F32)
    for half, source in enumerate((mine_ref, other_ref)):
        for block in range(4):
            part = source[block * 16 : block * 16 + 16].reshape(512, 256)
            total += jnp.sum(part * part, axis=0, keepdims=True)
    scale = 1.7 / jnp.sqrt(jnp.sum(total, axis=1, keepdims=True) + 1e-06)
    for half, source in enumerate((mine_ref, other_ref)):
        for block in range(4):
            rows, columns = slice(half * 512, half * 512 + 512), slice(block * 256, block * 256 + 256)
            part = source[block * 16 : block * 16 + 16].reshape(512, 256) * scale
            now_ref[rows, columns] = part
            high, low = split(part)
            hl_ref[0, 0, rows, columns] = high
            hl_ref[0, 1, rows, columns] = low

    def step(k, carry):
        old, new = lax.rem(k, 2), 1 - lax.rem(k, 2)
        high_ref, low_ref = hl_ref.at[old, 0], hl_ref.at[old, 1]
        for j in range(4):
            strip = slice(j * 256, j * 256 + 256)
            mixed_ref[:, strip] = mxu(high_ref[...], low_ref[strip], NT)
        for j in range(4):
            strip, below = slice(j * 256, j * 256 + 256), slice(j * 256, D)
            gram = mxu(high_ref[below], high_ref[strip], NT)
            gram += mixed_ref[below, strip] + mixed_ref[strip, below].T
            high, low = split(gram)
            gh_ref[below, strip] = high
            gl_ref[below, strip] = low
            if j < 3:
                high, low = split(gram[256:].T)
                gh_ref[strip, j * 256 + 256 : D] = high
                gl_ref[strip, j * 256 + 256 : D] = low
        for j in range(4):
            strip = slice(j * 256, j * 256 + 256)
            moved = dot3(gh_ref[...], gl_ref[...], high_ref[:, strip], low_ref[:, strip], NN)
            value = 1.5 * now_ref[:, strip] - 0.5 * moved
            now_ref[:, strip] = value
            high, low = split(value)
            hl_ref[new, 0, :, strip] = high
            hl_ref[new, 1, :, strip] = low
        return carry

    lax.fori_loop(0, NS_ITERS - 1, step, 0)
    last = (NS_ITERS - 1) % 2
    high_ref, low_ref = hl_ref.at[last, 0], hl_ref.at[last, 1]
    columns = pl.ds(pl.multiple_of(column // 4 * 128, 128), 128)
    now = []
    for z in range(4):
        for c in range(2):
            half = lax.rem(c + core, 2)
            rows = pl.ds(pl.multiple_of(half * 512 + y * 128 + z * 32, 32), 32)
            here = slice(z * 64 + c * 32, z * 64 + c * 32 + 32)
            tail_ref[0, here] = high_ref[rows]
            tail_ref[1, here] = low_ref[rows]
            now.append(now_ref[rows, columns])
    gram = dot3(tail_ref[0], tail_ref[1], high_ref[...], low_ref[...], NT)
    high, low = split(gram)
    moved = dot3(high, low, high_ref[:, columns], low_ref[:, columns], NN)
    turned_ref[...] = ((1.5 * jnp.concatenate(now, axis=0) - 0.5 * moved) * D**0.5).T
    out_ref[...] = turned_ref[pl.ds(pl.multiple_of(lax.rem(column, 4) * 32, 32), 32), :]


def newton_schulz(place, mine, other):
    return pl.pallas_call(
        iterate_kernel,
        out_shape=jax.ShapeDtypeStruct((32, 256), F32),
        in_specs=[SMEM, VMEM, VMEM],
        out_specs=VMEM,
        scratch_shapes=[
            pltpu.VMEM((D, D), F32),
            pltpu.VMEM((2, 2, D, D), BF16),
            pltpu.VMEM((D, D), BF16),
            pltpu.VMEM((D, D), BF16),
            pltpu.VMEM((2, 256, D), BF16),
            pltpu.VMEM((128, 256), F32),
            pltpu.VMEM((D, D), F32),
        ],
        compiler_params=grant(34),
        name="newton_schulz",
    )(place, mine, other)


def shards(points, codes, rotation):
    y, core = lax.axis_index("y"), lax.axis_index("core")
    own_row = lax.axis_index(ROWS)
    place = jnp.stack([y, core, own_row]).astype(jnp.int32)
    one, three = shift(codes, 1), shift(codes, 3)
    swapped = lax.ppermute(
        rotation, ("x", "y"), [(a * 4 + b, b * 4 + a) for a in range(4) for b in range(4)]
    )
    swapped, one, three = lax.optimization_barrier((swapped, one, three))
    pieces, two = spread_to(swapped, ("x", "z"), 16), shift(one, 1)
    pieces, two = lax.optimization_barrier((pieces, two))
    all_codes = [in_hbm(c) for c in (codes, one, two, three)]
    points = in_hbm(points)
    keep, give = code_sums(place, points, pieces, swap_core(pieces), all_codes)

    sums = keep + swap_core(give)
    sums = jnp.sum(lax.all_to_all(sums, CHIPS, 0, 0, tiled=True), axis=0)
    counts = sums[:, PAYLOAD - 128 :].reshape(1, K)
    sums = sums[:, : PAYLOAD - 128].reshape(2, 2, 4, 128).transpose(2, 0, 1, 3).reshape(SUB, K)
    centers = spread_to(sums / counts, CHIPS, 64)
    others = swap_core(centers)

    keep, give = cross_part(place, points, centers, others, all_codes)
    block = keep + swap_core(give)
    block = jnp.sum(lax.all_to_all(block, ("x", "z"), 0, 0, tiled=True), axis=0)
    whole = spread_to(block, CHIPS, 64)
    ours = lax.dynamic_slice_in_dim(centers, y * 16, 16, axis=0)
    theirs = lax.dynamic_slice_in_dim(others, y * 16, 16, axis=0)
    first, second = jnp.where(core == 0, ours, theirs), jnp.where(core == 0, theirs, ours)
    centroids = jnp.stack([first, second], axis=1).transpose(0, 1, 3, 2).reshape(32, K * SUB)
    whole, centroids = lax.optimization_barrier((whole, centroids))
    rotated = newton_schulz(place, whole, swap_core(whole))
    return (rotated, centroids)


def solution(mesh):
    grid = Mesh(mesh.devices.reshape(4, 4, 2, 4), ("x", "z", "core", "y"))
    in_specs = (P(ROWS, "y"), P("y", ROWS), P(ROWS, "y"))
    out_specs = (P(ROWS, "y"), P("y", None))
    return jax.shard_map(shards, mesh=grid, in_specs=in_specs, out_specs=out_specs, check_vma=False)
```
